32 devices in a mesh: row: 2 (over x), col: 4 (over z), layer: 4 (over y, core).
Axes of the slice: x: 2, y: 2, z: 4, core: 2. Of those that a mesh axis runs over, the one named last changes fastest.
Arguments:
- ks_owned: float32 [48, 16, 64, 64], P(('row', 'col'), 'layer'), may hold values from -0.4375 to 0.4375
- owned_rows: int32 [48], P(('row', 'col')), may hold values from -1 to 47, as said below
- left_cols: int32 [48, 16], P('row', 'layer'), may hold values from 0 to 47, as said below
- right_blocks: float32 [48, 16, 64, 64], P(('layer', 'row'), 'col'), may hold values from -6 to 6
- right_cols: int32 [48, 16], P('layer', 'col'), may hold values from 0 to 47, as said below
- kept_cols: int32 [48, 32], P('row', 'col'), may hold values from 0 to 47, as said below
Outputs:
- product_blocks: float32 [48, 32, 64, 64], P(('row', 'layer'), 'col')
The draws below stay inside these ranges and needn't reach their ends.
Inputs may be any that keep to these rules, and one draw needn't show every extreme that they name: `owned_rows`: slot s belongs to owner s // 6, at grid row (s // 6) // 4 and grid column (s // 6) % 4. Block row i belongs to cell i // 6, at grid row (i // 6) // 4 and grid column (i // 6) % 4. Every block row is held in exactly one slot, by an owner in its cell's grid column; all other slots hold -1. An owner holds at most 3 block rows of one cell, and in every draw some owner of every grid column holds 3 block rows of each cell of that column, 6 in all. `left_cols`: slots l * 4 to (l + 1) * 4 - 1 of each block row hold distinct block columns from l * 12 to (l + 1) * 12 - 1. `right_cols`: slots c * 4 to (c + 1) * 4 - 1 of each block row hold distinct block columns from c * 12 to (c + 1) * 12 - 1. `kept_cols`: slots c * 8 to (c + 1) * 8 - 1 of each block row hold distinct block columns from c * 12 to (c + 1) * 12 - 1.
All inputs are finite; a program needn't handle non-finite values.
Results may differ from the reference program's by a relative error of at most 0.0003.
Values sent between devices are 32-bit elements; how exact they have to be, the bound alone decides.
A program may use at most 128 MiB of HBM per device.

```python
import jax
import jax.numpy as jnp
from jax import lax

BS = 64
CELL_ROWS = 6
KAL = 4
KBC = 4
KCC = 8
GRID_ROWS = 2
GRID_COLS = 4
LAYERS = 4
NB = 48
INNER = 12
COLS = 12
KA = 16
KB = 16
SEND_CAP = 3
OWN_CAP = 6
HEAVY = 1


def column_sets(base_key, row_total, groups, spread, picks):
    key_list = jax.random.split(base_key, row_total * groups)
    chosen = jax.vmap(lambda single: jax.random.permutation(single, spread)[:picks])(key_list)
    chosen = chosen.reshape(row_total, groups, picks) + (jnp.arange(groups) * spread)[None, :, None]
    return chosen.reshape(row_total, groups * picks).astype(jnp.int32)


def draw_left_cols(key, part):
    return column_sets(jax.random.fold_in(key, 11), NB, LAYERS, INNER, KAL)


def draw_right_cols(key, part):
    return column_sets(jax.random.fold_in(key, 12), NB, GRID_COLS, COLS, KBC)


def draw_kept_cols(key, part):
    return column_sets(jax.random.fold_in(key, 13), NB, GRID_COLS, COLS, KCC)


def draw_owned_rows(key, part):
    first_key, second_key, third_key = jax.random.split(jax.random.fold_in(key, 21), 3)
    cell_total = GRID_ROWS * GRID_COLS
    row_index = jnp.arange(NB)
    cell_index = row_index // CELL_ROWS
    shuffle = jax.vmap(lambda single: jax.random.permutation(single, CELL_ROWS))(jax.random.split(first_key, cell_total))
    within = shuffle[cell_index, row_index % CELL_ROWS]
    grid_row = cell_index // GRID_COLS
    grid_col = cell_index % GRID_COLS
    heavy_rows = HEAVY * SEND_CAP
    is_heavy = within < heavy_rows
    light_rank = within - heavy_rows
    light_owner = HEAVY + (light_rank // SEND_CAP + grid_row) % (GRID_ROWS - HEAVY)
    local_owner = jnp.where(is_heavy, within // SEND_CAP, light_owner)
    position = grid_row * SEND_CAP + jnp.where(is_heavy, within % SEND_CAP, light_rank % SEND_CAP)
    owner_order = jax.vmap(lambda single: jax.random.permutation(single, GRID_ROWS))(jax.random.split(second_key, GRID_COLS))
    owner_index = owner_order[grid_col, local_owner] * GRID_COLS + grid_col
    slot_order = jax.vmap(lambda single: jax.random.permutation(single, OWN_CAP))(jax.random.split(third_key, cell_total))
    slot_index = owner_index * OWN_CAP + slot_order[owner_index, position]
    empty_slots = jnp.full((cell_total * OWN_CAP,), -1, jnp.int32)
    return empty_slots.at[slot_index].set(row_index.astype(jnp.int32))


def steps_of(key, extent, cuts, least, largest):
    def one(dim, parts):
        heights = jax.random.uniform(jax.random.fold_in(jax.random.fold_in(key, 6), dim), (parts,), jnp.float32, least / len(cuts), largest / len(cuts))
        return jnp.repeat(jnp.exp(heights), extent[dim] // parts).reshape((-1,) + (1,) * (len(extent) - dim - 1))

    factor_of = one(*cuts[0])
    for cut in cuts[1:]:
        factor_of = factor_of * one(*cut)
    return factor_of


def centred(stream_key, dims, scale, most, cuts=(), kind=jnp.bfloat16):
    array = jax.random.normal(stream_key, dims, jnp.float32) * scale
    if len(cuts) > 0:
        array = steps_of(stream_key, dims, cuts, -0.22, 0.18) * array
    return jnp.clip(array, min=-most, max=most).astype(kind)


def setup_inputs(seed: int = 0) -> dict:
    seeds = jax.random.split(jax.random.key(seed), 7)
    return {
        "ks_owned": centred(seeds[0], (GRID_ROWS * GRID_COLS * OWN_CAP, KA, BS, BS), (3 * BS) ** -0.5, 0.4375, ((0, 8), (1, 4)), jnp.float32),
        "owned_rows": draw_owned_rows(jax.random.fold_in(seeds[6], 71), 0),
        "left_cols": draw_left_cols(jax.random.fold_in(seeds[6], 71), 0),
        "right_blocks": centred(seeds[3], (NB, KB, BS, BS), 1.0, 6.0, ((0, 8), (1, 4)), jnp.float32),
        "right_cols": draw_right_cols(jax.random.fold_in(seeds[6], 71), 0),
        "kept_cols": draw_kept_cols(jax.random.fold_in(seeds[6], 71), 0),
    }


def reference(ks_owned, owned_rows, left_cols, right_blocks, right_cols, kept_cols):
    target = jnp.where(owned_rows >= 0, owned_rows, NB)
    left_blocks = jnp.zeros((NB,) + ks_owned.shape[1:], ks_owned.dtype).at[target].set(ks_owned, mode="drop")

    def row_product(packed_row):
        left_row, inner_ids, wanted = packed_row
        picked = right_blocks[inner_ids]
        picked_cols = right_cols[inner_ids]
        products = jnp.einsum("kab,klbc->klac", left_row, picked, precision=lax.Precision.HIGHEST)
        matches = (picked_cols[:, :, None] == wanted[None, None, :]).astype(left_row.dtype)
        return jnp.einsum("klq,klac->qac", matches, products, precision=lax.Precision.HIGHEST)

    return lax.map(row_product, (left_blocks, left_cols, kept_cols))
```

```python
import functools

import jax
import jax.numpy as jnp
from jax import lax
from jax.experimental import pallas as pl
from jax.experimental.pallas import tpu as pltpu
from jax.sharding import PartitionSpec as P

MESH = pl.DeviceIdType.MESH
LANES = 128
SUBLANES = 8
DENSE_BYTES = 8 << 20


def pack_rows(values, row_ids, groups, per_group, row_span):
    usable = row_ids >= 0
    target_group = jnp.where(usable, row_ids // row_span, groups)
    member = (target_group[:, None] == jnp.arange(groups)[None, :]).astype(jnp.int32)
    before = jnp.sum((jnp.cumsum(member, axis=0) - 1) * member, axis=1)
    target = jnp.where(usable, target_group * per_group + before, -1)
    chooser = target[None, :] == jnp.arange(groups * per_group)[:, None]
    packed = jnp.dot(chooser.astype(jnp.float32), values, precision=lax.Precision.HIGHEST)
    packed_ids = jnp.sum(jnp.where(chooser, row_ids[None, :] + 1, 0), axis=1) - 1
    return (packed, packed_ids.astype(jnp.float32))


def place_rows(arrived, arrived_ids, first_row, row_total):
    row_ids = arrived_ids.astype(jnp.int32)
    offset = row_ids - first_row
    chooser = (offset[None, :] == jnp.arange(row_total)[:, None]) & (row_ids >= 0)[None, :]
    return jnp.dot(chooser.astype(jnp.float32), arrived, precision=lax.Precision.HIGHEST)


def general_shards(ks_owned, owned_rows, left_cols, right_blocks, right_cols, kept_cols):
    row_count = lax.axis_size("row")
    col_count = lax.axis_size("col")
    owner_slots = ks_owned.shape[0]
    slot_count = ks_owned.shape[1]
    block_size = ks_owned.shape[2]
    send_limit = owner_slots // row_count
    panel_rows = left_cols.shape[0]
    cell_size = panel_rows // col_count
    my_row = lax.axis_index("row")
    flat_values = ks_owned.reshape(owner_slots, slot_count * block_size * block_size)
    packed, packed_ids = pack_rows(flat_values, owned_rows, row_count, send_limit, panel_rows)
    arrived, arrived_ids = (
        lax.all_to_all(packed, "row", split_axis=0, concat_axis=0, tiled=True),
        lax.all_to_all(packed_ids, "row", split_axis=0, concat_axis=0, tiled=True),
    )
    my_cell = my_row * col_count + lax.axis_index("col")
    cell_blocks = place_rows(arrived, arrived_ids, my_cell * cell_size, cell_size)
    left_panel = lax.all_gather(cell_blocks, "col", axis=0, tiled=True)
    right_panel = lax.all_gather(right_blocks, "row", axis=0, tiled=True)
    inner_rows = right_panel.shape[0]
    layer_start = lax.axis_index("layer") * inner_rows
    left_rows = left_panel.reshape(panel_rows, slot_count, block_size, block_size)
    local_cols = left_cols - layer_start
    picked = right_panel[local_cols]
    picked_cols = right_cols[local_cols]
    products = jnp.einsum("rkab,rklbc->rklac", left_rows, picked, precision=lax.Precision.HIGHEST)
    matches = (picked_cols[:, :, :, None] == kept_cols[:, None, None, :]).astype(jnp.float32)
    partial_value = jnp.einsum(
        "rklq,rklac->rqac", matches, products, precision=lax.Precision.HIGHEST
    )
    return lax.psum_scatter(partial_value, "layer", scatter_dimension=0, tiled=True)


def kernel(
    sizes,
    owned_ref,
    lcols_ref,
    rcols_ref,
    kept_ref,
    ks_ref,
    right_ref,
    out_ref,
    xsend,
    lbuf,
    rall,
    rpanel,
    r_hi,
    r_lo,
    lpanel,
    a_hi,
    a_lo,
    spread,
    partial,
    crecv,
    yrecv,
    x_ssem,
    r_ssem,
    z_ssem,
    c_ssem,
    y_ssem,
    l_rsem,
    r_rsem,
    c_rsem,
    y_rsem,
):
    nr, nc, nl = sizes
    r, c, l = lax.axis_index("row"), lax.axis_index("col"), lax.axis_index("layer")
    slots, kal, bs, _ = ks_ref.shape
    limit = slots // nr
    panel = lcols_ref.shape[0]
    cell = panel // nc
    rrows, kbc = right_ref.shape[:2]
    inner = rrows * nr
    kcc = kept_ref.shape[1]
    cols = r_hi.shape[1] // bs
    c0 = c * cols
    l0 = l * inner
    partner = l + 1 - 2 * lax.rem(l, 2)
    parity = lax.rem(l, 2)
    half = l // 2
    data_rows = limit * (kal // 2) * bs
    low = lax.broadcasted_iota(jnp.int32, (bs, LANES), 1) < bs

    barrier = pltpu.get_barrier_semaphore()
    expect = (nr - 1) + 1 + (nl // 2 - 1)
    for u in range(1, nr):
        pl.semaphore_signal(barrier, inc=1, device_id={"row": lax.rem(r + u, nr)}, device_id_type=MESH)
    pl.semaphore_signal(barrier, inc=1, device_id={"layer": partner}, device_id_type=MESH)
    for u in range(1, nl // 2):
        other = lax.rem(half + u, nl // 2) * 2 + parity
        pl.semaphore_signal(barrier, inc=1, device_id={"layer": other}, device_id_type=MESH)

    @pl.when(c > 0)
    def _():
        pl.semaphore_signal(barrier, inc=1, device_id={"col": c - 1}, device_id_type=MESH)

    @pl.when(c < nc - 1)
    def _():
        pl.semaphore_signal(barrier, inc=1, device_id={"col": c + 1}, device_id_type=MESH)

    expect = expect + jnp.where(c > 0, 1, 0) + jnp.where(c < nc - 1, 1, 0)

    ids = [owned_ref[s] for s in range(slots)]

    def pack_left(target, dst):
        first = target * panel
        inside = [jnp.logical_and(v >= first, v < first + panel) for v in ids]
        rank = jnp.int32(0)
        source = [jnp.int32(0)] * limit
        name = [jnp.int32(-1)] * limit
        for s in range(slots):
            for n in range(limit):
                hit = jnp.logical_and(inside[s], rank == n)
                source[n] = jnp.where(hit, s, source[n])
                name[n] = jnp.where(hit, ids[s], name[n])
            rank = rank + jnp.where(inside[s], 1, 0)
        for n in range(limit):
            for p in range(kal // 2):
                at = (n * (kal // 2) + p) * bs
                tile = jnp.concatenate([ks_ref[source[n], 2 * p], ks_ref[source[n], 2 * p + 1]], axis=-1)
                dst[pl.ds(at, bs), :] = tile
            dst[pl.ds(data_rows + n * SUBLANES, SUBLANES), :] = jnp.full((SUBLANES, LANES), name[n], jnp.int32).astype(jnp.float32)

    def x_copy(u):
        return pltpu.make_async_remote_copy(
            src_ref=xsend.at[u - 1],
            dst_ref=lbuf.at[c, r],
            send_sem=x_ssem.at[u - 1],
            recv_sem=l_rsem.at[c, r],
            device_id={"row": lax.rem(r + u, nr)},
            device_id_type=MESH,
        )

    def r_copy(u):
        return pltpu.make_async_remote_copy(
            src_ref=rall.at[r],
            dst_ref=rall.at[r],
            send_sem=r_ssem.at[u - 1],
            recv_sem=r_rsem.at[r],
            device_id={"row": lax.rem(r + u, nr)},
            device_id_type=MESH,
        )

    def z_copy(q, s, side):
        return pltpu.make_async_remote_copy(
            src_ref=lbuf.at[q, s],
            dst_ref=lbuf.at[q, s],
            send_sem=z_ssem.at[side, q, s],
            recv_sem=l_rsem.at[q, s],
            device_id={"col": c + 1 if side == 0 else c - 1},
            device_id_type=MESH,
        )

    def arrival(buf, sem):
        return pltpu.make_async_remote_copy(
            src_ref=buf,
            dst_ref=buf,
            send_sem=sem,
            recv_sem=sem,
            device_id={"layer": partner},
            device_id_type=MESH,
        )

    def both_sides(q, s, act):
        @pl.when(jnp.logical_and(q <= c, c < nc - 1))
        def _():
            act(z_copy(q, s, 0))

        @pl.when(jnp.logical_and(q >= c, c > 0))
        def _():
            act(z_copy(q, s, 1))

    start = lambda copy: copy.start()

    def order(t):
        near = jnp.minimum(c, nc - 1 - c)
        step = (t + 1) // 2
        paired = jnp.where(lax.rem(t, 2) == 1, c - step, c + step)
        single = jnp.where(c == near, c + (t - near), c - (t - near))
        return jnp.where(t <= 2 * near, paired, single)

    def forward(q, skip_own):
        for u in range(nr):
            s = lax.rem(r + u, nr)
            if skip_own and u == 0:
                continue
            arrival(lbuf.at[q, s], l_rsem.at[q, s]).wait_recv()
            both_sides(q, s, start)

    for u in range(1, nr):
        pack_left(lax.rem(r + u, nr), xsend.at[u - 1])
    pl.semaphore_wait(barrier, expect)
    for u in range(1, nr):
        x_copy(u).start()
    pack_left(r, lbuf.at[c, r])
    both_sides(c, r, start)
    for j in range(rrows):
        for p in range(kbc // 2):
            at = (j * (kbc // 2) + p) * bs
            rall[r, pl.ds(at, bs), :] = jnp.concatenate([right_ref[j, 2 * p], right_ref[j, 2 * p + 1]], axis=-1)
    for u in range(1, nr):
        r_copy(u).start()
    zero = jnp.zeros((bs, LANES), jnp.float32)

    def dense_right(s):
        def body(jj, carry):
            j = s * rrows + jj
            for p in range(kbc // 2):
                at = pl.multiple_of((jj * (kbc // 2) + p) * bs, bs)
                tile = rall[s, pl.ds(at, bs), :]
                rpanel[j, 2 * p] = tile
                rpanel[j, 2 * p + 1] = pltpu.roll(tile, bs, 1)
            rpanel[j, kbc] = zero
            names = [rcols_ref[j, k] - c0 for k in range(kbc)]
            for m in range(cols // 2):
                first, second = jnp.int32(kbc), jnp.int32(kbc)
                for k in range(kbc):
                    first = jnp.where(names[k] == 2 * m, k, first)
                    second = jnp.where(names[k] == 2 * m + 1, k ^ 1, second)
                tile = jnp.where(low, rpanel[j, first], rpanel[j, second])
                hi = tile.astype(jnp.bfloat16)
                at = pl.multiple_of(j * bs, bs)
                r_hi[pl.ds(at, bs), pl.ds(m * LANES, LANES)] = hi
                r_lo[pl.ds(at, bs), pl.ds(m * LANES, LANES)] = (tile - hi.astype(jnp.float32)).astype(jnp.bfloat16)
            return carry

        lax.fori_loop(0, rrows, body, 0)

    dense_right(r)
    forward(c, True)
    forward(order(jnp.int32(1)), False)
    for u in range(1, nr):
        s = lax.rem(r + u, nr)
        arrival(rall.at[s], r_rsem.at[s]).wait_recv()
        dense_right(s)

    width = 2 * LANES if (cols * bs) % (2 * LANES) == 0 else LANES
    cpair = kcc // 2

    def c_copy(q):
        return pltpu.make_async_remote_copy(
            src_ref=partial.at[q],
            dst_ref=crecv.at[q // 2],
            send_sem=c_ssem.at[q // 2],
            recv_sem=c_rsem.at[q // 2],
            device_id={"layer": partner},
            device_id_type=MESH,
        )

    def y_copy(q):
        return pltpu.make_async_remote_copy(
            src_ref=partial.at[q],
            dst_ref=yrecv.at[half],
            send_sem=y_ssem.at[q // 2],
            recv_sem=y_rsem.at[half],
            device_id={"layer": q},
            device_id_type=MESH,
        )

    def product(q):
        def place(i, carry):
            wanted = (r * panel + q * cell + i).astype(jnp.float32)
            tiles = [zero] * (kal // 2)
            for s in range(nr):
                for n in range(limit):
                    mark = lbuf[q, s, pl.ds(data_rows + n * SUBLANES, SUBLANES), :]
                    take = jnp.tile(mark == wanted, (bs // SUBLANES, 1))
                    for p in range(kal // 2):
                        at = (n * (kal // 2) + p) * bs
                        tiles[p] = jnp.where(take, lbuf[q, s, pl.ds(at, bs), :], tiles[p])
            for p in range(kal // 2):
                lpanel[i, 2 * p] = tiles[p]
                lpanel[i, 2 * p + 1] = pltpu.roll(tiles[p], bs, 1)
            lpanel[i, kal] = zero
            names = [lcols_ref[q * cell + i, k] - l0 for k in range(kal)]
            at = pl.multiple_of(i * bs, bs)
            for m in range(inner // 2):
                first, second = jnp.int32(kal), jnp.int32(kal)
                for k in range(kal):
                    first = jnp.where(names[k] == 2 * m, k, first)
                    second = jnp.where(names[k] == 2 * m + 1, k ^ 1, second)
                tile = jnp.where(low, lpanel[i, first], lpanel[i, second])
                hi = tile.astype(jnp.bfloat16)
                a_hi[pl.ds(at, bs), pl.ds(m * LANES, LANES)] = hi
                a_lo[pl.ds(at, bs), pl.ds(m * LANES, LANES)] = (tile - hi.astype(jnp.float32)).astype(jnp.bfloat16)
            return carry

        lax.fori_loop(0, cell, place, 0)
        dot = functools.partial(jnp.dot, preferred_element_type=jnp.float32)
        for n in range(cols * bs // width):
            at = pl.ds(n * width, width)
            value = dot(a_hi[...], r_lo[:, at]) + dot(a_lo[...], r_hi[:, at]) + dot(a_hi[...], r_hi[:, at])
            for h in range(width // LANES):
                m = n * (width // LANES) + h
                tile = value[:, h * LANES : (h + 1) * LANES]
                spread[2 * m] = tile
                spread[2 * m + 1] = pltpu.roll(tile, bs, 1)

        def keep(i, carry):
            at = pl.ds(pl.multiple_of(i * bs, bs), bs)
            for p in range(cpair):
                first = jnp.clip(kept_ref[q * cell + i, 2 * p] - c0, 0, cols - 1)
                second = jnp.clip(kept_ref[q * cell + i, 2 * p + 1] - c0, 0, cols - 1)
                second = second + 1 - 2 * lax.rem(second, 2)
                to = pl.multiple_of((i * cpair + p) * bs, bs)
                partial[q, pl.ds(to, bs), :] = jnp.where(low, spread[first, at, :], spread[second, at, :])
            return carry

        lax.fori_loop(0, cell, keep, 0)

    def step(t, carry):
        q = order(t)

        @pl.when(t >= 2)
        def _():
            forward(q, False)

        product(q)

        @pl.when(lax.rem(q, 2) != parity)
        def _():
            c_copy(q).start()

        @pl.when(lax.rem(q, 2) == parity)
        def _():
            arrival(crecv.at[q // 2], c_rsem.at[q // 2]).wait_recv()
            partial[q] = partial[q] + crecv[q // 2]

            @pl.when(q != l)
            def _():
                y_copy(q).start()

        return carry

    lax.fori_loop(0, nc, step, 0)

    for u in range(1, nl // 2):
        h = lax.rem(half + u, nl // 2)
        arrival(yrecv.at[h], y_rsem.at[h]).wait_recv()

    def finish(i, carry):
        for p in range(cpair):
            at = pl.ds(pl.multiple_of((i * cpair + p) * bs, bs), bs)
            tile = partial[l, at, :]
            for u in range(1, nl // 2):
                tile = tile + yrecv[lax.rem(half + u, nl // 2), at, :]
            out_ref[i, 2 * p] = tile[:, :bs]
            out_ref[i, 2 * p + 1] = tile[:, bs:]
        return carry

    lax.fori_loop(0, cell, finish, 0)

    wait = lambda copy: copy.wait_send()
    for u in range(1, nr):
        x_copy(u).wait_send()
        r_copy(u).wait_send()

    def drain(q, carry):
        for s in range(nr):
            both_sides(q, s, wait)

        @pl.when(lax.rem(q, 2) != parity)
        def _():
            c_copy(q).wait_send()

        @pl.when(jnp.logical_and(lax.rem(q, 2) == parity, q != l))
        def _():
            y_copy(q).wait_send()

        return carry

    lax.fori_loop(0, nc, drain, 0)


def fused_shards(sizes, ks_owned, owned_rows, left_cols, right_blocks, right_cols, kept_cols):
    nr, nc, nl = sizes
    slots, kal, bs, _ = ks_owned.shape
    limit = slots // nr
    panel = left_cols.shape[0]
    cell = panel // nc
    rrows, kbc = right_blocks.shape[:2]
    inner = rrows * nr
    kcc = kept_cols.shape[1]
    cols = inner * nl // nc
    chunk = limit * ((kal // 2) * bs + SUBLANES)
    share = cell * (kcc // 2) * bs
    f32, bf16 = jnp.float32, jnp.bfloat16
    smem = pl.BlockSpec(memory_space=pltpu.SMEM)
    vmem = pl.BlockSpec(memory_space=pltpu.VMEM)
    dma = pltpu.SemaphoreType.DMA
    return pl.pallas_call(
        functools.partial(kernel, sizes),
        out_shape=jax.ShapeDtypeStruct((cell, kcc, bs, bs), f32),
        in_specs=[smem] * 4 + [vmem] * 2,
        out_specs=vmem,
        scratch_shapes=[
            pltpu.VMEM((nr - 1, chunk, LANES), f32),
            pltpu.VMEM((nc, nr, chunk, LANES), f32),
            pltpu.VMEM((nr, rrows * (kbc // 2) * bs, LANES), f32),
            pltpu.VMEM((inner, kbc + 1, bs, LANES), f32),
            pltpu.VMEM((inner * bs, cols * bs), bf16),
            pltpu.VMEM((inner * bs, cols * bs), bf16),
            pltpu.VMEM((cell, kal + 1, bs, LANES), f32),
            pltpu.VMEM((cell * bs, inner * bs), bf16),
            pltpu.VMEM((cell * bs, inner * bs), bf16),
            pltpu.VMEM((cols, cell * bs, LANES), f32),
            pltpu.VMEM((nc, share, LANES), f32),
            pltpu.VMEM((nl // 2, share, LANES), f32),
            pltpu.VMEM((nl // 2, share, LANES), f32),
            dma((nr - 1,)),
            dma((nr - 1,)),
            dma((2, nc, nr)),
            dma((nl // 2,)),
            dma((nl // 2,)),
            dma((nc, nr)),
            dma((nr,)),
            dma((nl // 2,)),
            dma((nl // 2,)),
        ],
        compiler_params=pltpu.CompilerParams(
            collective_id=0, has_side_effects=True, vmem_limit_bytes=60 << 20
        ),
    )(owned_rows, left_cols, right_cols, kept_cols, ks_owned, right_blocks)


def solution(mesh):
    sizes = (mesh.shape["row"], mesh.shape["col"], mesh.shape["layer"])
    nr, nc, nl = sizes

    def shards(ks_owned, owned_rows, left_cols, right_blocks, right_cols, kept_cols):
        bs = ks_owned.shape[2]
        inner = right_cols.shape[0]
        cols = inner * nl // nc
        even = all(v % 2 == 0 for v in (ks_owned.shape[1], right_cols.shape[1], kept_cols.shape[1], inner, cols, nl))
        fits = 4 * inner * cols * bs * bs <= DENSE_BYTES
        if 2 * bs == LANES and even and fits and nc == nl and nc > 1 and nr > 1:
            return fused_shards(sizes, ks_owned, owned_rows, left_cols, right_blocks, right_cols, kept_cols)
        return general_shards(ks_owned, owned_rows, left_cols, right_blocks, right_cols, kept_cols)

    placed = (
        P(("row", "col"), "layer", None, None),
        P(("row", "col")),
        P("row", "layer"),
        P(("layer", "row"), "col", None, None),
        P("layer", "col"),
        P("row", "col"),
    )
    return jax.shard_map(
        shards,
        mesh=mesh,
        in_specs=placed,
        out_specs=P(("row", "layer"), "col", None, None),
        check_vma=False,
    )
```

```python
import functools

import jax
import jax.numpy as jnp
from jax import lax
from jax.experimental import pallas as pl
from jax.experimental.pallas import tpu as pltpu
from jax.sharding import PartitionSpec as P

MESH = pl.DeviceIdType.MESH
LANES = 128
SUBLANES = 8
DENSE_BYTES = 8 << 20


def pack_rows(values, row_ids, groups, per_group, row_span):
    usable = row_ids >= 0
    target_group = jnp.where(usable, row_ids // row_span, groups)
    member = (target_group[:, None] == jnp.arange(groups)[None, :]).astype(jnp.int32)
    before = jnp.sum((jnp.cumsum(member, axis=0) - 1) * member, axis=1)
    target = jnp.where(usable, target_group * per_group + before, -1)
    chooser = target[None, :] == jnp.arange(groups * per_group)[:, None]
    packed = jnp.dot(chooser.astype(jnp.float32), values, precision=lax.Precision.HIGHEST)
    packed_ids = jnp.sum(jnp.where(chooser, row_ids[None, :] + 1, 0), axis=1) - 1
    return (packed, packed_ids.astype(jnp.float32))


def place_rows(arrived, arrived_ids, first_row, row_total):
    row_ids = arrived_ids.astype(jnp.int32)
    offset = row_ids - first_row
    chooser = (offset[None, :] == jnp.arange(row_total)[:, None]) & (row_ids >= 0)[None, :]
    return jnp.dot(chooser.astype(jnp.float32), arrived, precision=lax.Precision.HIGHEST)


def general_shards(ks_owned, owned_rows, left_cols, right_blocks, right_cols, kept_cols):
    row_count = lax.axis_size("row")
    col_count = lax.axis_size("col")
    owner_slots = ks_owned.shape[0]
    slot_count = ks_owned.shape[1]
    block_size = ks_owned.shape[2]
    send_limit = owner_slots // row_count
    panel_rows = left_cols.shape[0]
    cell_size = panel_rows // col_count
    my_row = lax.axis_index("row")
    flat_values = ks_owned.reshape(owner_slots, slot_count * block_size * block_size)
    packed, packed_ids = pack_rows(flat_values, owned_rows, row_count, send_limit, panel_rows)
    arrived, arrived_ids = (
        lax.all_to_all(packed, "row", split_axis=0, concat_axis=0, tiled=True),
        lax.all_to_all(packed_ids, "row", split_axis=0, concat_axis=0, tiled=True),
    )
    my_cell = my_row * col_count + lax.axis_index("col")
    cell_blocks = place_rows(arrived, arrived_ids, my_cell * cell_size, cell_size)
    left_panel = lax.all_gather(cell_blocks, "col", axis=0, tiled=True)
    right_panel = lax.all_gather(right_blocks, "row", axis=0, tiled=True)
    inner_rows = right_panel.shape[0]
    layer_start = lax.axis_index("layer") * inner_rows
    left_rows = left_panel.reshape(panel_rows, slot_count, block_size, block_size)
    local_cols = left_cols - layer_start
    picked = right_panel[local_cols]
    picked_cols = right_cols[local_cols]
    products = jnp.einsum("rkab,rklbc->rklac", left_rows, picked, precision=lax.Precision.HIGHEST)
    matches = (picked_cols[:, :, :, None] == kept_cols[:, None, None, :]).astype(jnp.float32)
    partial_value = jnp.einsum(
        "rklq,rklac->rqac", matches, products, precision=lax.Precision.HIGHEST
    )
    return lax.psum_scatter(partial_value, "layer", scatter_dimension=0, tiled=True)


def kernel(
    sizes,
    owned_ref,
    lcols_ref,
    rcols_ref,
    kept_ref,
    ks_ref,
    right_ref,
    out_ref,
    ibuf,
    ids_smem,
    xsend,
    lbuf,
    rall,
    rpanel,
    r_hi,
    r_lo,
    lpanel,
    a_both,
    spread,
    partial,
    crecv,
    yrecv,
    i_ssem,
    i_rsem,
    t_sem,
    x_ssem,
    r_ssem,
    z_ssem,
    c_ssem,
    y_ssem,
    l_rsem,
    r_rsem,
    c_rsem,
    y_rsem,
):
    nr, nc, nl = sizes
    r, c, l = lax.axis_index("row"), lax.axis_index("col"), lax.axis_index("layer")
    slots, kal, bs, _ = ks_ref.shape
    limit = slots // nr
    panel = lcols_ref.shape[1]
    cell = panel // nc
    rrows, kbc = right_ref.shape[:2]
    inner = rrows * nr
    kcc = kept_ref.shape[0]
    cols = r_hi.shape[1] // bs
    c0 = c * cols
    l0 = l * inner
    partner = l + 1 - 2 * lax.rem(l, 2)
    parity = lax.rem(l, 2)
    half = l // 2
    low = lax.broadcasted_iota(jnp.int32, (bs, LANES), 1) < bs

    barrier = pltpu.get_barrier_semaphore()
    def peer(k):
        at = lax.rem(r * nc + c + k, nr * nc)
        return {"row": at // nc, "col": lax.rem(at, nc)}

    for k in range(1, nr * nc):
        pl.semaphore_signal(barrier, inc=1, device_id=peer(k), device_id_type=MESH)
    pl.semaphore_signal(barrier, inc=1, device_id={"layer": partner}, device_id_type=MESH)
    for u in range(1, nl // 2):
        other = lax.rem(half + u, nl // 2) * 2 + parity
        pl.semaphore_signal(barrier, inc=1, device_id={"layer": other}, device_id_type=MESH)
    expect = (nr * nc - 1) + 1 + (nl // 2 - 1)

    ids = [owned_ref[s] for s in range(slots)]

    def pack_left(target, dst):
        first = target * panel
        inside = [jnp.logical_and(v >= first, v < first + panel) for v in ids]
        rank = jnp.int32(0)
        source = [jnp.int32(0)] * limit
        for s in range(slots):
            for n in range(limit):
                hit = jnp.logical_and(inside[s], rank == n)
                source[n] = jnp.where(hit, s, source[n])
            rank = rank + jnp.where(inside[s], 1, 0)
        for n in range(limit):
            for p in range(kal // 2):
                at = (n * (kal // 2) + p) * bs
                tile = jnp.concatenate([ks_ref[source[n], 2 * p], ks_ref[source[n], 2 * p + 1]], axis=-1)
                dst[pl.ds(at, bs), :] = tile

    def i_copy(k):
        return pltpu.make_async_remote_copy(
            src_ref=ibuf.at[r, c],
            dst_ref=ibuf.at[r, c],
            send_sem=i_ssem.at[k - 1],
            recv_sem=i_rsem.at[r, c],
            device_id=peer(k),
            device_id_type=MESH,
        )

    def names_of(q, s):
        first = r * panel
        rank = jnp.int32(0)
        name = [first] * limit
        for v in range(slots):
            value = ids_smem[s, q, v, 0]
            inside = jnp.logical_and(value >= first, value < first + panel)
            for n in range(limit):
                name[n] = jnp.where(jnp.logical_and(inside, rank == n), value, name[n])
            rank = rank + jnp.where(inside, 1, 0)
        return [jnp.clip(v - first, 0, panel - 1) for v in name], rank

    def x_copy(u):
        return pltpu.make_async_remote_copy(
            src_ref=xsend.at[u - 1],
            dst_ref=lbuf.at[c, r],
            send_sem=x_ssem.at[u - 1],
            recv_sem=l_rsem.at[c, r],
            device_id={"row": lax.rem(r + u, nr)},
            device_id_type=MESH,
        )

    def r_copy(u):
        return pltpu.make_async_remote_copy(
            src_ref=rall.at[r],
            dst_ref=rall.at[r],
            send_sem=r_ssem.at[u - 1],
            recv_sem=r_rsem.at[r],
            device_id={"row": lax.rem(r + u, nr)},
            device_id_type=MESH,
        )

    def z_copy(q, s, side):
        return pltpu.make_async_remote_copy(
            src_ref=lbuf.at[q, s],
            dst_ref=lbuf.at[q, s],
            send_sem=z_ssem.at[side, q, s],
            recv_sem=l_rsem.at[q, s],
            device_id={"col": c + 1 if side == 0 else c - 1},
            device_id_type=MESH,
        )

    def arrival(buf, sem):
        return pltpu.make_async_remote_copy(
            src_ref=buf,
            dst_ref=buf,
            send_sem=sem,
            recv_sem=sem,
            device_id={"layer": partner},
            device_id_type=MESH,
        )

    def both_sides(q, s, act):
        @pl.when(jnp.logical_and(q <= c, c < nc - 1))
        def _():
            act(z_copy(q, s, 0))

        @pl.when(jnp.logical_and(q >= c, c > 0))
        def _():
            act(z_copy(q, s, 1))

    start = lambda copy: copy.start()

    def order(t):
        near = jnp.minimum(c, nc - 1 - c)
        step = (t + 1) // 2
        paired = jnp.where(lax.rem(t, 2) == 1, c - step, c + step)
        single = jnp.where(c == near, c + (t - near), c - (t - near))
        return jnp.where(t <= 2 * near, paired, single)

    def passes(q):
        return jnp.logical_or(jnp.logical_and(q < c, c < nc - 1), jnp.logical_and(q > c, c > 0))

    def forward(t):
        q = order(jnp.int32(t))

        @pl.when(passes(q))
        def _():
            for u in range(nr):
                s = lax.rem(r + u, nr)
                arrival(lbuf.at[q, s], l_rsem.at[q, s]).wait_recv()
                both_sides(q, s, start)

    for u in range(1, nr):
        pack_left(lax.rem(r + u, nr), xsend.at[u - 1])
    mark = jnp.full(ibuf.shape[2:], -1, jnp.int32)
    level = lax.broadcasted_iota(jnp.int32, ibuf.shape[2:], 0)
    for s in range(slots):
        mark = jnp.where(level == s, ids[s], mark)
    ibuf[r, c] = mark
    pl.semaphore_wait(barrier, expect)
    for u in range(1, nr):
        x_copy(u).start()
    pack_left(r, lbuf.at[c, r])
    both_sides(c, r, start)
    for k in range(1, nr * nc):
        i_copy(k).start()
    for j in range(rrows):
        for p in range(kbc // 2):
            at = (j * (kbc // 2) + p) * bs
            rall[r, pl.ds(at, bs), :] = jnp.concatenate([right_ref[j, 2 * p], right_ref[j, 2 * p + 1]], axis=-1)
    for u in range(1, nr):
        r_copy(u).start()
    zero = jnp.zeros((bs, LANES), jnp.float32)

    def dense_right(s):
        def body(jj, carry):
            j = s * rrows + jj
            for p in range(kbc // 2):
                at = pl.multiple_of((jj * (kbc // 2) + p) * bs, bs)
                tile = rall[s, pl.ds(at, bs), :]
                rpanel[j, 2 * p] = tile
                rpanel[j, 2 * p + 1] = pltpu.roll(tile, bs, 1)
            rpanel[j, kbc] = zero
            names = [rcols_ref[k, j] - c0 for k in range(kbc)]
            for m in range(cols // 2):
                first, second = jnp.int32(kbc), jnp.int32(kbc)
                for k in range(kbc):
                    first = jnp.where(names[k] == 2 * m, k, first)
                    second = jnp.where(names[k] == 2 * m + 1, k ^ 1, second)
                tile = jnp.where(low, rpanel[j, first], rpanel[j, second])
                hi = tile.astype(jnp.bfloat16)
                at = pl.multiple_of(j * bs, bs)
                r_hi[pl.ds(at, bs), pl.ds(m * LANES, LANES)] = hi
                r_lo[pl.ds(at, bs), pl.ds(m * LANES, LANES)] = (tile - hi.astype(jnp.float32)).astype(jnp.bfloat16)
            return carry

        lax.fori_loop(0, rrows, body, 0)

    dense_right(r)
    for u in range(1, nr):
        s = lax.rem(r + u, nr)
        arrival(lbuf.at[c, s], l_rsem.at[c, s]).wait_recv()
        both_sides(c, s, start)
    for k in range(1, nr * nc):
        at = lax.rem(r * nc + c + k, nr * nc)
        s, q = at // nc, lax.rem(at, nc)
        arrival(ibuf.at[s, q], i_rsem.at[s, q]).wait_recv()
    table = pltpu.make_async_copy(ibuf, ids_smem, t_sem)
    table.start()
    table.wait()
    for t in range(1, min(3, nc)):
        forward(t)
    for u in range(1, nr):
        s = lax.rem(r + u, nr)
        arrival(rall.at[s], r_rsem.at[s]).wait_recv()
        dense_right(s)

    width = 2 * LANES if (cols * bs) % (2 * LANES) == 0 else LANES
    cpair = kcc // 2

    def c_copy(q, s):
        return pltpu.make_async_remote_copy(
            src_ref=partial.at[q, s],
            dst_ref=crecv.at[q // 2, s],
            send_sem=c_ssem.at[q // 2, s],
            recv_sem=c_rsem.at[q // 2, s],
            device_id={"layer": partner},
            device_id_type=MESH,
        )

    def y_copy(q, s):
        return pltpu.make_async_remote_copy(
            src_ref=partial.at[q, s],
            dst_ref=yrecv.at[half, s],
            send_sem=y_ssem.at[q // 2, s],
            recv_sem=y_rsem.at[half, s],
            device_id={"layer": q},
            device_id_type=MESH,
        )

    def chosen(table, k, q, row):
        value = table[k, q * cell]
        for i in range(1, cell):
            value = jnp.where(row == q * cell + i, table[k, q * cell + i], value)
        return value

    def product(q, s):
        rows, _ = names_of(q, s)
        for n in range(limit):
            for p in range(kal // 2):
                tile = lbuf[q, s, pl.ds((n * (kal // 2) + p) * bs, bs), :]
                lpanel[n, 2 * p] = tile
                lpanel[n, 2 * p + 1] = pltpu.roll(tile, bs, 1)
            lpanel[n, kal] = zero
            names = [chosen(lcols_ref, k, q, rows[n]) - l0 for k in range(kal)]
            for m in range(inner // 2):
                first, second = jnp.int32(kal), jnp.int32(kal)
                for k in range(kal):
                    first = jnp.where(names[k] == 2 * m, k, first)
                    second = jnp.where(names[k] == 2 * m + 1, k ^ 1, second)
                tile = jnp.where(low, lpanel[n, first], lpanel[n, second])
                hi = tile.astype(jnp.bfloat16)
                at = pl.ds(m * LANES, LANES)
                a_both[n * bs : (n + 1) * bs, at] = hi
                a_both[(limit + n) * bs : (limit + n + 1) * bs, at] = (tile - hi.astype(jnp.float32)).astype(jnp.bfloat16)
        tall = limit * bs
        dot = functools.partial(jnp.dot, preferred_element_type=jnp.float32)
        for n in range(cols * bs // width):
            at = pl.ds(n * width, width)
            value = dot(a_both[...], r_hi[:, at])
            value = value[:tall] + value[tall:] + dot(a_both[:tall, :], r_lo[:, at])
            for h in range(width // LANES):
                m = n * (width // LANES) + h
                tile = value[:, h * LANES : (h + 1) * LANES]
                spread[2 * m] = tile
                spread[2 * m + 1] = pltpu.roll(tile, bs, 1)
        for n in range(limit):
            at = pl.ds(n * bs, bs)
            for p in range(cpair):
                first = jnp.clip(chosen(kept_ref, 2 * p, q, rows[n]) - c0, 0, cols - 1)
                second = jnp.clip(chosen(kept_ref, 2 * p + 1, q, rows[n]) - c0, 0, cols - 1)
                second = second + 1 - 2 * lax.rem(second, 2)
                partial[q, s, n * cpair + p] = jnp.where(low, spread[first, at, :], spread[second, at, :])

    def step(w, carry):
        t = w // nr
        u = lax.rem(w, nr)
        q = order(t)
        s = lax.rem(r + u, nr)

        @pl.when(jnp.logical_and(q != c, jnp.logical_not(passes(q))))
        def _():
            arrival(lbuf.at[q, s], l_rsem.at[q, s]).wait_recv()

        product(q, s)

        @pl.when(lax.rem(q, 2) != parity)
        def _():
            c_copy(q, s).start()

        @pl.when(jnp.logical_and(u == nr - 1, t + 3 < nc))
        def _():
            forward(t + 3)

        @pl.when(lax.rem(q, 2) == parity)
        def _():
            arrival(crecv.at[q // 2, s], c_rsem.at[q // 2, s]).wait_recv()
            partial[q, s] = partial[q, s] + crecv[q // 2, s]

            @pl.when(q != l)
            def _():
                y_copy(q, s).start()

        return carry

    lax.fori_loop(0, nc * nr, step, 0)

    source = [jnp.int32(0)] * cell
    spot = [jnp.int32(0)] * cell
    for s in range(nr):
        rows, count = names_of(l, s)
        for n in range(limit):
            for i in range(cell):
                hit = jnp.logical_and(rows[n] == l * cell + i, n < count)
                source[i] = jnp.where(hit, s, source[i])
                spot[i] = jnp.where(hit, n * cpair, spot[i])
    for u in range(1, nl // 2):
        h = lax.rem(half + u, nl // 2)
        for v in range(nr):
            s = lax.rem(r + v, nr)
            arrival(yrecv.at[h, s], y_rsem.at[h, s]).wait_recv()
    for i in range(cell):
        for p in range(cpair):
            tile = partial[l, source[i], spot[i] + p]
            for u in range(1, nl // 2):
                tile = tile + yrecv[lax.rem(half + u, nl // 2), source[i], spot[i] + p]
            out_ref[i, 2 * p] = tile[:, :bs]
            out_ref[i, 2 * p + 1] = tile[:, bs:]

    wait = lambda copy: copy.wait_send()
    for u in range(1, nr):
        x_copy(u).wait_send()
        r_copy(u).wait_send()
    for k in range(1, nr * nc):
        i_copy(k).wait_send()

    def drain(q, carry):
        for s in range(nr):
            both_sides(q, s, wait)

        @pl.when(lax.rem(q, 2) != parity)
        def _():
            for s in range(nr):
                c_copy(q, s).wait_send()

        @pl.when(jnp.logical_and(lax.rem(q, 2) == parity, q != l))
        def _():
            for s in range(nr):
                y_copy(q, s).wait_send()

        return carry

    lax.fori_loop(0, nc, drain, 0)


def fused_shards(sizes, ks_owned, owned_rows, left_cols, right_blocks, right_cols, kept_cols):
    nr, nc, nl = sizes
    slots, kal, bs, _ = ks_owned.shape
    limit = slots // nr
    panel = left_cols.shape[0]
    cell = panel // nc
    rrows, kbc = right_blocks.shape[:2]
    inner = rrows * nr
    kcc = kept_cols.shape[1]
    cols = inner * nl // nc
    chunk = limit * (kal // 2) * bs
    share = limit * (kcc // 2)
    f32, bf16 = jnp.float32, jnp.bfloat16
    smem = pl.BlockSpec(memory_space=pltpu.SMEM)
    vmem = pl.BlockSpec(memory_space=pltpu.VMEM)
    dma = pltpu.SemaphoreType.DMA
    return pl.pallas_call(
        functools.partial(kernel, sizes),
        out_shape=jax.ShapeDtypeStruct((cell, kcc, bs, bs), f32),
        in_specs=[smem] * 4 + [vmem] * 2,
        out_specs=vmem,
        scratch_shapes=[
            pltpu.VMEM((nr, nc, -(-slots // SUBLANES) * SUBLANES, LANES), jnp.int32),
            pltpu.SMEM((nr, nc, -(-slots // SUBLANES) * SUBLANES, LANES), jnp.int32),
            pltpu.VMEM((nr - 1, chunk, LANES), f32),
            pltpu.VMEM((nc, nr, chunk, LANES), f32),
            pltpu.VMEM((nr, rrows * (kbc // 2) * bs, LANES), f32),
            pltpu.VMEM((inner, kbc + 1, bs, LANES), f32),
            pltpu.VMEM((inner * bs, cols * bs), bf16),
            pltpu.VMEM((inner * bs, cols * bs), bf16),
            pltpu.VMEM((limit, kal + 1, bs, LANES), f32),
            pltpu.VMEM((2 * limit * bs, inner * bs), bf16),
            pltpu.VMEM((cols, limit * bs, LANES), f32),
            pltpu.VMEM((nc, nr, share, bs, LANES), f32),
            pltpu.VMEM((nl // 2, nr, share, bs, LANES), f32),
            pltpu.VMEM((nl // 2, nr, share, bs, LANES), f32),
            dma((nr * nc - 1,)),
            dma((nr, nc)),
            dma(()),
            dma((nr - 1,)),
            dma((nr - 1,)),
            dma((2, nc, nr)),
            dma((nl // 2, nr)),
            dma((nl // 2, nr)),
            dma((nc, nr)),
            dma((nr,)),
            dma((nl // 2, nr)),
            dma((nl // 2, nr)),
        ],
        compiler_params=pltpu.CompilerParams(
            collective_id=0, has_side_effects=True, vmem_limit_bytes=60 << 20
        ),
    )(owned_rows, left_cols.T, right_cols.T, kept_cols.T, ks_owned, right_blocks)


def solution(mesh):
    sizes = (mesh.shape["row"], mesh.shape["col"], mesh.shape["layer"])
    nr, nc, nl = sizes

    def shards(ks_owned, owned_rows, left_cols, right_blocks, right_cols, kept_cols):
        bs = ks_owned.shape[2]
        inner = right_cols.shape[0]
        cols = inner * nl // nc
        even = all(v % 2 == 0 for v in (ks_owned.shape[1], right_cols.shape[1], kept_cols.shape[1], inner, cols, nl))
        fits = 4 * inner * cols * bs * bs <= DENSE_BYTES
        if 2 * bs == LANES and even and fits and nc == nl and nc > 1 and nr > 1:
            return fused_shards(sizes, ks_owned, owned_rows, left_cols, right_blocks, right_cols, kept_cols)
        return general_shards(ks_owned, owned_rows, left_cols, right_blocks, right_cols, kept_cols)

    placed = (
        P(("row", "col"), "layer", None, None),
        P(("row", "col")),
        P("row", "layer"),
        P(("layer", "row"), "col", None, None),
        P("layer", "col"),
        P("row", "col"),
    )
    return jax.shard_map(
        shards,
        mesh=mesh,
        in_specs=placed,
        out_specs=P(("row", "layer"), "col", None, None),
        check_vma=False,
    )
```

```python
import functools

import jax
import jax.numpy as jnp
from jax import lax
from jax.experimental import pallas as pl
from jax.experimental.pallas import tpu as pltpu
from jax.sharding import PartitionSpec as P

MESH = pl.DeviceIdType.MESH
LANES = 128
SUBLANES = 8
DENSE_BYTES = 8 << 20


def pack_rows(values, row_ids, groups, per_group, row_span):
    usable = row_ids >= 0
    target_group = jnp.where(usable, row_ids // row_span, groups)
    member = (target_group[:, None] == jnp.arange(groups)[None, :]).astype(jnp.int32)
    before = jnp.sum((jnp.cumsum(member, axis=0) - 1) * member, axis=1)
    target = jnp.where(usable, target_group * per_group + before, -1)
    chooser = target[None, :] == jnp.arange(groups * per_group)[:, None]
    packed = jnp.dot(chooser.astype(jnp.float32), values, precision=lax.Precision.HIGHEST)
    packed_ids = jnp.sum(jnp.where(chooser, row_ids[None, :] + 1, 0), axis=1) - 1
    return (packed, packed_ids.astype(jnp.float32))


def place_rows(arrived, arrived_ids, first_row, row_total):
    row_ids = arrived_ids.astype(jnp.int32)
    offset = row_ids - first_row
    chooser = (offset[None, :] == jnp.arange(row_total)[:, None]) & (row_ids >= 0)[None, :]
    return jnp.dot(chooser.astype(jnp.float32), arrived, precision=lax.Precision.HIGHEST)


def general_shards(ks_owned, owned_rows, left_cols, right_blocks, right_cols, kept_cols):
    row_count = lax.axis_size("row")
    col_count = lax.axis_size("col")
    owner_slots = ks_owned.shape[0]
    slot_count = ks_owned.shape[1]
    block_size = ks_owned.shape[2]
    send_limit = owner_slots // row_count
    panel_rows = left_cols.shape[0]
    cell_size = panel_rows // col_count
    my_row = lax.axis_index("row")
    flat_values = ks_owned.reshape(owner_slots, slot_count * block_size * block_size)
    packed, packed_ids = pack_rows(flat_values, owned_rows, row_count, send_limit, panel_rows)
    arrived, arrived_ids = (
        lax.all_to_all(packed, "row", split_axis=0, concat_axis=0, tiled=True),
        lax.all_to_all(packed_ids, "row", split_axis=0, concat_axis=0, tiled=True),
    )
    my_cell = my_row * col_count + lax.axis_index("col")
    cell_blocks = place_rows(arrived, arrived_ids, my_cell * cell_size, cell_size)
    left_panel = lax.all_gather(cell_blocks, "col", axis=0, tiled=True)
    right_panel = lax.all_gather(right_blocks, "row", axis=0, tiled=True)
    inner_rows = right_panel.shape[0]
    layer_start = lax.axis_index("layer") * inner_rows
    left_rows = left_panel.reshape(panel_rows, slot_count, block_size, block_size)
    local_cols = left_cols - layer_start
    picked = right_panel[local_cols]
    picked_cols = right_cols[local_cols]
    products = jnp.einsum("rkab,rklbc->rklac", left_rows, picked, precision=lax.Precision.HIGHEST)
    matches = (picked_cols[:, :, :, None] == kept_cols[:, None, None, :]).astype(jnp.float32)
    partial_value = jnp.einsum(
        "rklq,rklac->rqac", matches, products, precision=lax.Precision.HIGHEST
    )
    return lax.psum_scatter(partial_value, "layer", scatter_dimension=0, tiled=True)


def kernel(
    sizes,
    owned_ref,
    lcols_ref,
    rcols_ref,
    kept_ref,
    ks_ref,
    right_ref,
    out_ref,
    ibuf,
    ids_smem,
    xsend,
    lbuf,
    rall,
    rpanel,
    r_hi,
    r_lo,
    lpanel,
    a_both,
    spread,
    partial,
    crecv,
    yrecv,
    i_ssem,
    i_rsem,
    t_sem,
    x_ssem,
    r_ssem,
    z_ssem,
    c_ssem,
    y_ssem,
    l_rsem,
    r_rsem,
    c_rsem,
    y_rsem,
):
    nr, nc, nl = sizes
    r, c, l = lax.axis_index("row"), lax.axis_index("col"), lax.axis_index("layer")
    slots, kal, bs, _ = ks_ref.shape
    limit = slots // nr
    panel = lcols_ref.shape[1]
    cell = panel // nc
    rrows, kbc = right_ref.shape[:2]
    inner = rrows * nr
    kcc = kept_ref.shape[0]
    cols = r_hi.shape[1] // bs
    c0 = c * cols
    l0 = l * inner
    partner = l + 1 - 2 * lax.rem(l, 2)
    parity = lax.rem(l, 2)
    half = l // 2
    low = lax.broadcasted_iota(jnp.int32, (bs, LANES), 1) < bs

    barrier = pltpu.get_barrier_semaphore()
    def peer(k):
        at = lax.rem(r * nc + c + k, nr * nc)
        return {"row": at // nc, "col": lax.rem(at, nc)}

    for k in range(1, nr * nc):
        pl.semaphore_signal(barrier, inc=1, device_id=peer(k), device_id_type=MESH)
    pl.semaphore_signal(barrier, inc=1, device_id={"layer": partner}, device_id_type=MESH)
    for u in range(1, nl // 2):
        other = lax.rem(half + u, nl // 2) * 2 + parity
        pl.semaphore_signal(barrier, inc=1, device_id={"layer": other}, device_id_type=MESH)
    expect = (nr * nc - 1) + 1 + (nl // 2 - 1)

    ids = [owned_ref[s] for s in range(slots)]

    def pack_left(target, dst):
        first = target * panel
        inside = [jnp.logical_and(v >= first, v < first + panel) for v in ids]
        rank = jnp.int32(0)
        source = [jnp.int32(0)] * limit
        for s in range(slots):
            for n in range(limit):
                hit = jnp.logical_and(inside[s], rank == n)
                source[n] = jnp.where(hit, s, source[n])
            rank = rank + jnp.where(inside[s], 1, 0)
        for n in range(limit):
            for p in range(kal // 2):
                at = (n * (kal // 2) + p) * bs
                tile = jnp.concatenate([ks_ref[source[n], 2 * p], ks_ref[source[n], 2 * p + 1]], axis=-1)
                dst[pl.ds(at, bs), :] = tile

    def i_copy(k):
        return pltpu.make_async_remote_copy(
            src_ref=ibuf.at[r, c],
            dst_ref=ibuf.at[r, c],
            send_sem=i_ssem.at[k - 1],
            recv_sem=i_rsem.at[r, c],
            device_id=peer(k),
            device_id_type=MESH,
        )

    def names_of(q, s):
        first = r * panel
        rank = jnp.int32(0)
        name = [first] * limit
        for v in range(slots):
            value = ids_smem[s, q, v, 0]
            inside = jnp.logical_and(value >= first, value < first + panel)
            for n in range(limit):
                name[n] = jnp.where(jnp.logical_and(inside, rank == n), value, name[n])
            rank = rank + jnp.where(inside, 1, 0)
        return [jnp.clip(v - first, 0, panel - 1) for v in name], rank

    def x_copy(u):
        return pltpu.make_async_remote_copy(
            src_ref=xsend.at[u - 1],
            dst_ref=lbuf.at[c, r],
            send_sem=x_ssem.at[u - 1],
            recv_sem=l_rsem.at[c, r],
            device_id={"row": lax.rem(r + u, nr)},
            device_id_type=MESH,
        )

    def r_copy(u):
        return pltpu.make_async_remote_copy(
            src_ref=rall.at[r],
            dst_ref=rall.at[r],
            send_sem=r_ssem.at[u - 1],
            recv_sem=r_rsem.at[r],
            device_id={"row": lax.rem(r + u, nr)},
            device_id_type=MESH,
        )

    def z_copy(q, s, side):
        return pltpu.make_async_remote_copy(
            src_ref=lbuf.at[q, s],
            dst_ref=lbuf.at[q, s],
            send_sem=z_ssem.at[side, q, s],
            recv_sem=l_rsem.at[q, s],
            device_id={"col": c + 1 if side == 0 else c - 1},
            device_id_type=MESH,
        )

    def arrival(buf, sem):
        return pltpu.make_async_remote_copy(
            src_ref=buf,
            dst_ref=buf,
            send_sem=sem,
            recv_sem=sem,
            device_id={"layer": partner},
            device_id_type=MESH,
        )

    def both_sides(q, s, act):
        @pl.when(jnp.logical_and(q <= c, c < nc - 1))
        def _():
            act(z_copy(q, s, 0))

        @pl.when(jnp.logical_and(q >= c, c > 0))
        def _():
            act(z_copy(q, s, 1))

    start = lambda copy: copy.start()

    def order(t):
        near = jnp.minimum(c, nc - 1 - c)
        step = (t + 1) // 2
        paired = jnp.where(lax.rem(t, 2) == 1, c - step, c + step)
        single = jnp.where(c == near, c + (t - near), c - (t - near))
        return jnp.where(t <= 2 * near, paired, single)

    def passes(q):
        return jnp.logical_or(jnp.logical_and(q < c, c < nc - 1), jnp.logical_and(q > c, c > 0))

    def forward(t, u):
        q = order(t)
        s = lax.rem(r + u, nr)

        @pl.when(passes(q))
        def _():
            arrival(lbuf.at[q, s], l_rsem.at[q, s]).wait_recv()
            both_sides(q, s, start)

    for u in range(1, nr):
        pack_left(lax.rem(r + u, nr), xsend.at[u - 1])
    mark = jnp.full(ibuf.shape[2:], -1, jnp.int32)
    level = lax.broadcasted_iota(jnp.int32, ibuf.shape[2:], 0)
    for s in range(slots):
        mark = jnp.where(level == s, ids[s], mark)
    ibuf[r, c] = mark
    pl.semaphore_wait(barrier, expect)
    for u in range(1, nr):
        x_copy(u).start()
    pack_left(r, lbuf.at[c, r])
    both_sides(c, r, start)
    for k in range(1, nr * nc):
        i_copy(k).start()
    for j in range(rrows):
        for p in range(kbc // 2):
            at = (j * (kbc // 2) + p) * bs
            rall[r, pl.ds(at, bs), :] = jnp.concatenate([right_ref[j, 2 * p], right_ref[j, 2 * p + 1]], axis=-1)
    for u in range(1, nr):
        r_copy(u).start()
    zero = jnp.zeros((bs, LANES), jnp.float32)

    def dense_right(s):
        def body(jj, carry):
            j = s * rrows + jj
            for p in range(kbc // 2):
                at = pl.multiple_of((jj * (kbc // 2) + p) * bs, bs)
                tile = rall[s, pl.ds(at, bs), :]
                rpanel[j, 2 * p] = tile
                rpanel[j, 2 * p + 1] = pltpu.roll(tile, bs, 1)
            rpanel[j, kbc] = zero
            names = [rcols_ref[k, j] - c0 for k in range(kbc)]
            for m in range(cols // 2):
                first, second = jnp.int32(kbc), jnp.int32(kbc)
                for k in range(kbc):
                    first = jnp.where(names[k] == 2 * m, k, first)
                    second = jnp.where(names[k] == 2 * m + 1, k ^ 1, second)
                tile = jnp.where(low, rpanel[j, first], rpanel[j, second])
                hi = tile.astype(jnp.bfloat16)
                at = pl.multiple_of(j * bs, bs)
                r_hi[pl.ds(at, bs), pl.ds(m * LANES, LANES)] = hi
                r_lo[pl.ds(at, bs), pl.ds(m * LANES, LANES)] = (tile - hi.astype(jnp.float32)).astype(jnp.bfloat16)
            return carry

        lax.fori_loop(0, rrows, body, 0)

    dense_right(r)
    for u in range(1, nr):
        s = lax.rem(r + u, nr)
        arrival(lbuf.at[c, s], l_rsem.at[c, s]).wait_recv()
        both_sides(c, s, start)
    for u in range(nr):
        for t in range(1, min(3, nc)):
            forward(jnp.int32(t), u)
    for k in range(1, nr * nc):
        at = lax.rem(r * nc + c + k, nr * nc)
        s, q = at // nc, lax.rem(at, nc)
        arrival(ibuf.at[s, q], i_rsem.at[s, q]).wait_recv()
    table = pltpu.make_async_copy(ibuf, ids_smem, t_sem)
    table.start()
    table.wait()
    for u in range(1, nr):
        s = lax.rem(r + u, nr)
        arrival(rall.at[s], r_rsem.at[s]).wait_recv()
    if nc > 3:
        forward(jnp.int32(3), 0)
    for u in range(1, nr):
        dense_right(lax.rem(r + u, nr))

    width = 2 * LANES if (cols * bs) % (2 * LANES) == 0 else LANES
    cpair = kcc // 2

    def c_copy(q, s):
        return pltpu.make_async_remote_copy(
            src_ref=partial.at[q, s],
            dst_ref=crecv.at[q // 2, s],
            send_sem=c_ssem.at[q // 2, s],
            recv_sem=c_rsem.at[q // 2, s],
            device_id={"layer": partner},
            device_id_type=MESH,
        )

    def y_copy(q, s):
        return pltpu.make_async_remote_copy(
            src_ref=partial.at[q, s],
            dst_ref=yrecv.at[half, s],
            send_sem=y_ssem.at[q // 2, s],
            recv_sem=y_rsem.at[half, s],
            device_id={"layer": q},
            device_id_type=MESH,
        )

    def chosen(table, k, q, row):
        value = table[k, q * cell]
        for i in range(1, cell):
            value = jnp.where(row == q * cell + i, table[k, q * cell + i], value)
        return value

    def plan(q, s):
        rows, _ = names_of(q, s)
        left, kept = [], []
        for n in range(limit):
            names = [chosen(lcols_ref, k, q, rows[n]) - l0 for k in range(kal)]
            picks = []
            for m in range(inner // 2):
                first, second = jnp.int32(kal), jnp.int32(kal)
                for k in range(kal):
                    first = jnp.where(names[k] == 2 * m, k, first)
                    second = jnp.where(names[k] == 2 * m + 1, k ^ 1, second)
                picks.append((first, second))
            left.append(picks)
            picks = []
            for p in range(cpair):
                first = jnp.clip(chosen(kept_ref, 2 * p, q, rows[n]) - c0, 0, cols - 1)
                second = jnp.clip(chosen(kept_ref, 2 * p + 1, q, rows[n]) - c0, 0, cols - 1)
                picks.append((first, second + 1 - 2 * lax.rem(second, 2)))
            kept.append(picks)
        return left, kept

    def product(q, s, left, kept):
        for n in range(limit):
            for p in range(kal // 2):
                tile = lbuf[q, s, pl.ds((n * (kal // 2) + p) * bs, bs), :]
                lpanel[n, 2 * p] = tile
                lpanel[n, 2 * p + 1] = pltpu.roll(tile, bs, 1)
            lpanel[n, kal] = zero
            for m in range(inner // 2):
                first, second = left[n][m]
                tile = jnp.where(low, lpanel[n, first], lpanel[n, second])
                hi = tile.astype(jnp.bfloat16)
                at = pl.ds(m * LANES, LANES)
                a_both[n * bs : (n + 1) * bs, at] = hi
                a_both[(limit + n) * bs : (limit + n + 1) * bs, at] = (tile - hi.astype(jnp.float32)).astype(jnp.bfloat16)
        tall = limit * bs
        dot = functools.partial(jnp.dot, preferred_element_type=jnp.float32)
        for n in range(cols * bs // width):
            at = pl.ds(n * width, width)
            value = dot(a_both[...], r_hi[:, at])
            value = value[:tall] + value[tall:] + dot(a_both[:tall, :], r_lo[:, at])
            for h in range(width // LANES):
                m = n * (width // LANES) + h
                tile = value[:, h * LANES : (h + 1) * LANES]
                spread[2 * m] = tile
                spread[2 * m + 1] = pltpu.roll(tile, bs, 1)
        for n in range(limit):
            at = pl.ds(n * bs, bs)
            for p in range(cpair):
                first, second = kept[n][p]
                partial[q, s, n * cpair + p] = jnp.where(low, spread[first, at, :], spread[second, at, :])

    def step(w, carry):
        t = w // nr
        u = lax.rem(w, nr)
        q = order(t)
        s = lax.rem(r + u, nr)

        left, kept = plan(q, s)

        @pl.when(jnp.logical_and(q != c, jnp.logical_not(passes(q))))
        def _():
            arrival(lbuf.at[q, s], l_rsem.at[q, s]).wait_recv()

        product(q, s, left, kept)

        @pl.when(lax.rem(q, 2) != parity)
        def _():
            c_copy(q, s).start()

        ahead = w + 3 * nr + 1

        @pl.when(ahead < nc * nr)
        def _():
            forward(ahead // nr, lax.rem(ahead, nr))

        @pl.when(lax.rem(q, 2) == parity)
        def _():
            arrival(crecv.at[q // 2, s], c_rsem.at[q // 2, s]).wait_recv()
            partial[q, s] = partial[q, s] + crecv[q // 2, s]

            @pl.when(q != l)
            def _():
                y_copy(q, s).start()

        return carry

    lax.fori_loop(0, nc * nr, step, 0)

    source = [jnp.int32(0)] * cell
    spot = [jnp.int32(0)] * cell
    for s in range(nr):
        rows, count = names_of(l, s)
        for n in range(limit):
            for i in range(cell):
                hit = jnp.logical_and(rows[n] == l * cell + i, n < count)
                source[i] = jnp.where(hit, s, source[i])
                spot[i] = jnp.where(hit, n * cpair, spot[i])
    for u in range(1, nl // 2):
        h = lax.rem(half + u, nl // 2)
        for v in range(nr):
            s = lax.rem(r + v, nr)
            arrival(yrecv.at[h, s], y_rsem.at[h, s]).wait_recv()
    for i in range(cell):
        for p in range(cpair):
            tile = partial[l, source[i], spot[i] + p]
            for u in range(1, nl // 2):
                tile = tile + yrecv[lax.rem(half + u, nl // 2), source[i], spot[i] + p]
            out_ref[i, 2 * p] = tile[:, :bs]
            out_ref[i, 2 * p + 1] = tile[:, bs:]

    wait = lambda copy: copy.wait_send()
    for u in range(1, nr):
        x_copy(u).wait_send()
        r_copy(u).wait_send()
    for k in range(1, nr * nc):
        i_copy(k).wait_send()

    def drain(q, carry):
        for s in range(nr):
            both_sides(q, s, wait)

        @pl.when(lax.rem(q, 2) != parity)
        def _():
            for s in range(nr):
                c_copy(q, s).wait_send()

        @pl.when(jnp.logical_and(lax.rem(q, 2) == parity, q != l))
        def _():
            for s in range(nr):
                y_copy(q, s).wait_send()

        return carry

    lax.fori_loop(0, nc, drain, 0)


def fused_shards(sizes, ks_owned, owned_rows, left_cols, right_blocks, right_cols, kept_cols):
    nr, nc, nl = sizes
    slots, kal, bs, _ = ks_owned.shape
    limit = slots // nr
    panel = left_cols.shape[0]
    cell = panel // nc
    rrows, kbc = right_blocks.shape[:2]
    inner = rrows * nr
    kcc = kept_cols.shape[1]
    cols = inner * nl // nc
    chunk = limit * (kal // 2) * bs
    share = limit * (kcc // 2)
    f32, bf16 = jnp.float32, jnp.bfloat16
    smem = pl.BlockSpec(memory_space=pltpu.SMEM)
    vmem = pl.BlockSpec(memory_space=pltpu.VMEM)
    dma = pltpu.SemaphoreType.DMA
    return pl.pallas_call(
        functools.partial(kernel, sizes),
        out_shape=jax.ShapeDtypeStruct((cell, kcc, bs, bs), f32),
        in_specs=[smem] * 4 + [vmem] * 2,
        out_specs=vmem,
        scratch_shapes=[
            pltpu.VMEM((nr, nc, -(-slots // SUBLANES) * SUBLANES, LANES), jnp.int32),
            pltpu.SMEM((nr, nc, -(-slots // SUBLANES) * SUBLANES, LANES), jnp.int32),
            pltpu.VMEM((nr - 1, chunk, LANES), f32),
            pltpu.VMEM((nc, nr, chunk, LANES), f32),
            pltpu.VMEM((nr, rrows * (kbc // 2) * bs, LANES), f32),
            pltpu.VMEM((inner, kbc + 1, bs, LANES), f32),
            pltpu.VMEM((inner * bs, cols * bs), bf16),
            pltpu.VMEM((inner * bs, cols * bs), bf16),
            pltpu.VMEM((limit, kal + 1, bs, LANES), f32),
            pltpu.VMEM((2 * limit * bs, inner * bs), bf16),
            pltpu.VMEM((cols, limit * bs, LANES), f32),
            pltpu.VMEM((nc, nr, share, bs, LANES), f32),
            pltpu.VMEM((nl // 2, nr, share, bs, LANES), f32),
            pltpu.VMEM((nl // 2, nr, share, bs, LANES), f32),
            dma((nr * nc - 1,)),
            dma((nr, nc)),
            dma(()),
            dma((nr - 1,)),
            dma((nr - 1,)),
            dma((2, nc, nr)),
            dma((nl // 2, nr)),
            dma((nl // 2, nr)),
            dma((nc, nr)),
            dma((nr,)),
            dma((nl // 2, nr)),
            dma((nl // 2, nr)),
        ],
        compiler_params=pltpu.CompilerParams(
            collective_id=0, has_side_effects=True, vmem_limit_bytes=60 << 20
        ),
    )(owned_rows, left_cols.T, right_cols.T, kept_cols.T, ks_owned, right_blocks)


def solution(mesh):
    sizes = (mesh.shape["row"], mesh.shape["col"], mesh.shape["layer"])
    nr, nc, nl = sizes

    def shards(ks_owned, owned_rows, left_cols, right_blocks, right_cols, kept_cols):
        bs = ks_owned.shape[2]
        inner = right_cols.shape[0]
        cols = inner * nl // nc
        even = all(v % 2 == 0 for v in (ks_owned.shape[1], right_cols.shape[1], kept_cols.shape[1], inner, cols, nl))
        fits = 4 * inner * cols * bs * bs <= DENSE_BYTES
        if 2 * bs == LANES and even and fits and nc == nl and nc > 1 and nr > 1:
            return fused_shards(sizes, ks_owned, owned_rows, left_cols, right_blocks, right_cols, kept_cols)
        return general_shards(ks_owned, owned_rows, left_cols, right_blocks, right_cols, kept_cols)

    placed = (
        P(("row", "col"), "layer", None, None),
        P(("row", "col")),
        P("row", "layer"),
        P(("layer", "row"), "col", None, None),
        P("layer", "col"),
        P("row", "col"),
    )
    return jax.shard_map(
        shards,
        mesh=mesh,
        in_specs=placed,
        out_specs=P(("row", "layer"), "col", None, None),
        check_vma=False,
    )
```

```python
import functools

import jax
import jax.numpy as jnp
from jax import lax
from jax.experimental import pallas as pl
from jax.experimental.pallas import tpu as pltpu
from jax.sharding import PartitionSpec as P

MESH = pl.DeviceIdType.MESH
LANES = 128
SUBLANES = 8
DENSE_BYTES = 8 << 20


def pack_rows(values, row_ids, groups, per_group, row_span):
    usable = row_ids >= 0
    target_group = jnp.where(usable, row_ids // row_span, groups)
    member = (target_group[:, None] == jnp.arange(groups)[None, :]).astype(jnp.int32)
    before = jnp.sum((jnp.cumsum(member, axis=0) - 1) * member, axis=1)
    target = jnp.where(usable, target_group * per_group + before, -1)
    chooser = target[None, :] == jnp.arange(groups * per_group)[:, None]
    packed = jnp.dot(chooser.astype(jnp.float32), values, precision=lax.Precision.HIGHEST)
    packed_ids = jnp.sum(jnp.where(chooser, row_ids[None, :] + 1, 0), axis=1) - 1
    return (packed, packed_ids.astype(jnp.float32))


def place_rows(arrived, arrived_ids, first_row, row_total):
    row_ids = arrived_ids.astype(jnp.int32)
    offset = row_ids - first_row
    chooser = (offset[None, :] == jnp.arange(row_total)[:, None]) & (row_ids >= 0)[None, :]
    return jnp.dot(chooser.astype(jnp.float32), arrived, precision=lax.Precision.HIGHEST)


def general_shards(ks_owned, owned_rows, left_cols, right_blocks, right_cols, kept_cols):
    row_count = lax.axis_size("row")
    col_count = lax.axis_size("col")
    owner_slots = ks_owned.shape[0]
    slot_count = ks_owned.shape[1]
    block_size = ks_owned.shape[2]
    send_limit = owner_slots // row_count
    panel_rows = left_cols.shape[0]
    cell_size = panel_rows // col_count
    my_row = lax.axis_index("row")
    flat_values = ks_owned.reshape(owner_slots, slot_count * block_size * block_size)
    packed, packed_ids = pack_rows(flat_values, owned_rows, row_count, send_limit, panel_rows)
    arrived, arrived_ids = (
        lax.all_to_all(packed, "row", split_axis=0, concat_axis=0, tiled=True),
        lax.all_to_all(packed_ids, "row", split_axis=0, concat_axis=0, tiled=True),
    )
    my_cell = my_row * col_count + lax.axis_index("col")
    cell_blocks = place_rows(arrived, arrived_ids, my_cell * cell_size, cell_size)
    left_panel = lax.all_gather(cell_blocks, "col", axis=0, tiled=True)
    right_panel = lax.all_gather(right_blocks, "row", axis=0, tiled=True)
    inner_rows = right_panel.shape[0]
    layer_start = lax.axis_index("layer") * inner_rows
    left_rows = left_panel.reshape(panel_rows, slot_count, block_size, block_size)
    local_cols = left_cols - layer_start
    picked = right_panel[local_cols]
    picked_cols = right_cols[local_cols]
    products = jnp.einsum("rkab,rklbc->rklac", left_rows, picked, precision=lax.Precision.HIGHEST)
    matches = (picked_cols[:, :, :, None] == kept_cols[:, None, None, :]).astype(jnp.float32)
    partial_value = jnp.einsum(
        "rklq,rklac->rqac", matches, products, precision=lax.Precision.HIGHEST
    )
    return lax.psum_scatter(partial_value, "layer", scatter_dimension=0, tiled=True)


def kernel(
    sizes,
    owned_ref,
    lcols_ref,
    rcols_ref,
    kept_ref,
    ks_ref,
    right_ref,
    out_ref,
    ibuf,
    ids_smem,
    plans,
    xsend,
    lbuf,
    rall,
    rpanel,
    r_hi,
    r_lo,
    lpanel,
    a_both,
    spread,
    partial,
    crecv,
    yrecv,
    i_ssem,
    i_rsem,
    t_sem,
    x_ssem,
    r_ssem,
    z_ssem,
    c_ssem,
    y_ssem,
    l_rsem,
    r_rsem,
    c_rsem,
    y_rsem,
):
    nr, nc, nl = sizes
    r, c, l = lax.axis_index("row"), lax.axis_index("col"), lax.axis_index("layer")
    slots, kal, bs, _ = ks_ref.shape
    limit = slots // nr
    panel = lcols_ref.shape[1]
    cell = panel // nc
    rrows, kbc = right_ref.shape[:2]
    inner = rrows * nr
    kcc = kept_ref.shape[0]
    cols = r_hi.shape[1] // bs
    c0 = c * cols
    l0 = l * inner
    partner = l + 1 - 2 * lax.rem(l, 2)
    parity = lax.rem(l, 2)
    half = l // 2
    low = lax.broadcasted_iota(jnp.int32, (bs, LANES), 1) < bs

    barrier = pltpu.get_barrier_semaphore()
    def peer(k):
        at = lax.rem(r * nc + c + k, nr * nc)
        return {"row": at // nc, "col": lax.rem(at, nc)}

    for k in range(1, nr * nc):
        pl.semaphore_signal(barrier, inc=1, device_id=peer(k), device_id_type=MESH)
    pl.semaphore_signal(barrier, inc=1, device_id={"layer": partner}, device_id_type=MESH)
    for u in range(1, nl // 2):
        other = lax.rem(half + u, nl // 2) * 2 + parity
        pl.semaphore_signal(barrier, inc=1, device_id={"layer": other}, device_id_type=MESH)
    expect = (nr * nc - 1) + 1 + (nl // 2 - 1)

    ids = [owned_ref[s] for s in range(slots)]

    def pack_left(target, dst):
        first = target * panel
        inside = [jnp.logical_and(v >= first, v < first + panel) for v in ids]
        rank = jnp.int32(0)
        source = [jnp.int32(0)] * limit
        for s in range(slots):
            for n in range(limit):
                hit = jnp.logical_and(inside[s], rank == n)
                source[n] = jnp.where(hit, s, source[n])
            rank = rank + jnp.where(inside[s], 1, 0)
        for n in range(limit):
            for p in range(kal // 2):
                at = (n * (kal // 2) + p) * bs
                tile = jnp.concatenate([ks_ref[source[n], 2 * p], ks_ref[source[n], 2 * p + 1]], axis=-1)
                dst[pl.ds(at, bs), :] = tile

    def i_copy(k):
        return pltpu.make_async_remote_copy(
            src_ref=ibuf.at[r, c],
            dst_ref=ibuf.at[r, c],
            send_sem=i_ssem.at[k - 1],
            recv_sem=i_rsem.at[r, c],
            device_id=peer(k),
            device_id_type=MESH,
        )

    def names_of(q, s):
        first = r * panel
        rank = jnp.int32(0)
        name = [first] * limit
        for v in range(slots):
            value = ids_smem[s, q, v, 0]
            inside = jnp.logical_and(value >= first, value < first + panel)
            for n in range(limit):
                name[n] = jnp.where(jnp.logical_and(inside, rank == n), value, name[n])
            rank = rank + jnp.where(inside, 1, 0)
        return [jnp.clip(v - first, 0, panel - 1) for v in name], rank

    def x_copy(u):
        return pltpu.make_async_remote_copy(
            src_ref=xsend.at[u - 1],
            dst_ref=lbuf.at[c, r],
            send_sem=x_ssem.at[u - 1],
            recv_sem=l_rsem.at[c, r],
            device_id={"row": lax.rem(r + u, nr)},
            device_id_type=MESH,
        )

    def r_copy(u):
        return pltpu.make_async_remote_copy(
            src_ref=rall.at[r],
            dst_ref=rall.at[r],
            send_sem=r_ssem.at[u - 1],
            recv_sem=r_rsem.at[r],
            device_id={"row": lax.rem(r + u, nr)},
            device_id_type=MESH,
        )

    def z_copy(q, s, side):
        return pltpu.make_async_remote_copy(
            src_ref=lbuf.at[q, s],
            dst_ref=lbuf.at[q, s],
            send_sem=z_ssem.at[side, q, s],
            recv_sem=l_rsem.at[q, s],
            device_id={"col": c + 1 if side == 0 else c - 1},
            device_id_type=MESH,
        )

    def arrival(buf, sem):
        return pltpu.make_async_remote_copy(
            src_ref=buf,
            dst_ref=buf,
            send_sem=sem,
            recv_sem=sem,
            device_id={"layer": partner},
            device_id_type=MESH,
        )

    def both_sides(q, s, act):
        @pl.when(jnp.logical_and(q <= c, c < nc - 1))
        def _():
            act(z_copy(q, s, 0))

        @pl.when(jnp.logical_and(q >= c, c > 0))
        def _():
            act(z_copy(q, s, 1))

    start = lambda copy: copy.start()

    def order(t):
        near = jnp.minimum(c, nc - 1 - c)
        step = (t + 1) // 2
        paired = jnp.where(lax.rem(t, 2) == 1, c - step, c + step)
        single = jnp.where(c == near, c + (t - near), c - (t - near))
        return jnp.where(t <= 2 * near, paired, single)

    def passes(q):
        return jnp.logical_or(jnp.logical_and(q < c, c < nc - 1), jnp.logical_and(q > c, c > 0))

    def forward(t, u):
        q = order(t)
        s = lax.rem(r + u, nr)

        @pl.when(passes(q))
        def _():
            arrival(lbuf.at[q, s], l_rsem.at[q, s]).wait_recv()
            both_sides(q, s, start)

    for u in range(1, nr):
        pack_left(lax.rem(r + u, nr), xsend.at[u - 1])
    mark = jnp.full(ibuf.shape[2:], -1, jnp.int32)
    level = lax.broadcasted_iota(jnp.int32, ibuf.shape[2:], 0)
    for s in range(slots):
        mark = jnp.where(level == s, ids[s], mark)
    ibuf[r, c] = mark
    pl.semaphore_wait(barrier, expect)
    for u in range(1, nr):
        x_copy(u).start()
    pack_left(r, lbuf.at[c, r])
    both_sides(c, r, start)
    for k in range(1, nr * nc):
        i_copy(k).start()
    for j in range(rrows):
        for p in range(kbc // 2):
            at = (j * (kbc // 2) + p) * bs
            rall[r, pl.ds(at, bs), :] = jnp.concatenate([right_ref[j, 2 * p], right_ref[j, 2 * p + 1]], axis=-1)
    for u in range(1, nr):
        r_copy(u).start()
    zero = jnp.zeros((bs, LANES), jnp.float32)

    def dense_right(s):
        def body(jj, carry):
            j = s * rrows + jj
            for p in range(kbc // 2):
                at = pl.multiple_of((jj * (kbc // 2) + p) * bs, bs)
                tile = rall[s, pl.ds(at, bs), :]
                rpanel[j, 2 * p] = tile
                rpanel[j, 2 * p + 1] = pltpu.roll(tile, bs, 1)
            rpanel[j, kbc] = zero
            names = [rcols_ref[k, j] - c0 for k in range(kbc)]
            for m in range(cols // 2):
                first, second = jnp.int32(kbc), jnp.int32(kbc)
                for k in range(kbc):
                    first = jnp.where(names[k] == 2 * m, k, first)
                    second = jnp.where(names[k] == 2 * m + 1, k ^ 1, second)
                tile = jnp.where(low, rpanel[j, first], rpanel[j, second])
                hi = tile.astype(jnp.bfloat16)
                at = pl.multiple_of(j * bs, bs)
                r_hi[pl.ds(at, bs), pl.ds(m * LANES, LANES)] = hi
                r_lo[pl.ds(at, bs), pl.ds(m * LANES, LANES)] = (tile - hi.astype(jnp.float32)).astype(jnp.bfloat16)
            return carry

        lax.fori_loop(0, rrows, body, 0)

    dense_right(r)
    for u in range(1, nr):
        s = lax.rem(r + u, nr)
        arrival(lbuf.at[c, s], l_rsem.at[c, s]).wait_recv()
        both_sides(c, s, start)
    cpair = kcc // 2

    def chosen(table, k, q, row):
        value = table[k, q * cell]
        for i in range(1, cell):
            value = jnp.where(row == q * cell + i, table[k, q * cell + i], value)
        return value

    def plan(q, s):
        rows, _ = names_of(q, s)
        left, kept = [], []
        for n in range(limit):
            names = [chosen(lcols_ref, k, q, rows[n]) - l0 for k in range(kal)]
            picks = []
            for m in range(inner // 2):
                first, second = jnp.int32(kal), jnp.int32(kal)
                for k in range(kal):
                    first = jnp.where(names[k] == 2 * m, k, first)
                    second = jnp.where(names[k] == 2 * m + 1, k ^ 1, second)
                picks.append((first, second))
            left.append(picks)
            picks = []
            for p in range(cpair):
                first = jnp.clip(chosen(kept_ref, 2 * p, q, rows[n]) - c0, 0, cols - 1)
                second = jnp.clip(chosen(kept_ref, 2 * p + 1, q, rows[n]) - c0, 0, cols - 1)
                picks.append((first, second + 1 - 2 * lax.rem(second, 2)))
            kept.append(picks)
        return left, kept

    for u in range(nr):
        for t in range(1, min(3, nc)):
            forward(jnp.int32(t), u)
    for k in range(1, nr * nc):
        at = lax.rem(r * nc + c + k, nr * nc)
        s, q = at // nc, lax.rem(at, nc)
        arrival(ibuf.at[s, q], i_rsem.at[s, q]).wait_recv()
    table = pltpu.make_async_copy(ibuf, ids_smem, t_sem)
    table.start()
    table.wait()

    def prepare(w, carry):
        left, kept = plan(order(w // nr), lax.rem(r + lax.rem(w, nr), nr))
        values = [v for row in left + kept for pair in row for v in pair]
        for k, v in enumerate(values):
            plans[w, k] = v
        return carry

    lax.fori_loop(0, nc * nr, prepare, 0)
    for u in range(1, nr):
        s = lax.rem(r + u, nr)
        arrival(rall.at[s], r_rsem.at[s]).wait_recv()
    for u in range(1, nr):
        dense_right(lax.rem(r + u, nr))

    width = 2 * LANES if (cols * bs) % (2 * LANES) == 0 else LANES

    def c_copy(q, s):
        return pltpu.make_async_remote_copy(
            src_ref=partial.at[q, s],
            dst_ref=crecv.at[q // 2, s],
            send_sem=c_ssem.at[q // 2, s],
            recv_sem=c_rsem.at[q // 2, s],
            device_id={"layer": partner},
            device_id_type=MESH,
        )

    def y_copy(q, s):
        return pltpu.make_async_remote_copy(
            src_ref=partial.at[q, s],
            dst_ref=yrecv.at[half, s],
            send_sem=y_ssem.at[q // 2, s],
            recv_sem=y_rsem.at[half, s],
            device_id={"layer": q},
            device_id_type=MESH,
        )

    def product(q, s, left, kept):
        for n in range(limit):
            for p in range(kal // 2):
                tile = lbuf[q, s, pl.ds((n * (kal // 2) + p) * bs, bs), :]
                lpanel[n, 2 * p] = tile
                lpanel[n, 2 * p + 1] = pltpu.roll(tile, bs, 1)
            lpanel[n, kal] = zero
            for m in range(inner // 2):
                first, second = left[n][m]
                tile = jnp.where(low, lpanel[n, first], lpanel[n, second])
                hi = tile.astype(jnp.bfloat16)
                at = pl.ds(m * LANES, LANES)
                a_both[n * bs : (n + 1) * bs, at] = hi
                a_both[(limit + n) * bs : (limit + n + 1) * bs, at] = (tile - hi.astype(jnp.float32)).astype(jnp.bfloat16)
        tall = limit * bs
        dot = functools.partial(jnp.dot, preferred_element_type=jnp.float32)
        for n in range(cols * bs // width):
            at = pl.ds(n * width, width)
            value = dot(a_both[...], r_hi[:, at])
            value = value[:tall] + value[tall:] + dot(a_both[:tall, :], r_lo[:, at])
            for h in range(width // LANES):
                m = n * (width // LANES) + h
                tile = value[:, h * LANES : (h + 1) * LANES]
                spread[2 * m] = tile
                spread[2 * m + 1] = pltpu.roll(tile, bs, 1)
        for n in range(limit):
            at = pl.ds(n * bs, bs)
            for p in range(cpair):
                first, second = kept[n][p]
                partial[q, s, n * cpair + p] = jnp.where(low, spread[first, at, :], spread[second, at, :])

    def step(w, carry):
        t = w // nr
        u = lax.rem(w, nr)
        q = order(t)
        s = lax.rem(r + u, nr)

        @pl.when(jnp.logical_and(q != c, jnp.logical_not(passes(q))))
        def _():
            arrival(lbuf.at[q, s], l_rsem.at[q, s]).wait_recv()

        pair = lambda k: (plans[w, k], plans[w, k + 1])
        left = [[pair(n * inner + 2 * m) for m in range(inner // 2)] for n in range(limit)]
        kept = [[pair(limit * inner + n * kcc + 2 * p) for p in range(cpair)] for n in range(limit)]
        product(q, s, left, kept)

        @pl.when(lax.rem(q, 2) != parity)
        def _():
            c_copy(q, s).start()

        @pl.when(t + 3 < nc)
        def _():
            forward(t + 3, u)

        @pl.when(lax.rem(q, 2) == parity)
        def _():
            arrival(crecv.at[q // 2, s], c_rsem.at[q // 2, s]).wait_recv()
            partial[q, s] = partial[q, s] + crecv[q // 2, s]

            @pl.when(q != l)
            def _():
                y_copy(q, s).start()

        return carry

    lax.fori_loop(0, nc * nr, step, 0)

    source = [jnp.int32(0)] * cell
    spot = [jnp.int32(0)] * cell
    for s in range(nr):
        rows, count = names_of(l, s)
        for n in range(limit):
            for i in range(cell):
                hit = jnp.logical_and(rows[n] == l * cell + i, n < count)
                source[i] = jnp.where(hit, s, source[i])
                spot[i] = jnp.where(hit, n * cpair, spot[i])
    for u in range(1, nl // 2):
        h = lax.rem(half + u, nl // 2)
        for v in range(nr):
            s = lax.rem(r + v, nr)
            arrival(yrecv.at[h, s], y_rsem.at[h, s]).wait_recv()
    for i in range(cell):
        for p in range(cpair):
            tile = partial[l, source[i], spot[i] + p]
            for u in range(1, nl // 2):
                tile = tile + yrecv[lax.rem(half + u, nl // 2), source[i], spot[i] + p]
            out_ref[i, 2 * p] = tile[:, :bs]
            out_ref[i, 2 * p + 1] = tile[:, bs:]

    wait = lambda copy: copy.wait_send()
    for u in range(1, nr):
        x_copy(u).wait_send()
        r_copy(u).wait_send()
    for k in range(1, nr * nc):
        i_copy(k).wait_send()

    def drain(q, carry):
        for s in range(nr):
            both_sides(q, s, wait)

        @pl.when(lax.rem(q, 2) != parity)
        def _():
            for s in range(nr):
                c_copy(q, s).wait_send()

        @pl.when(jnp.logical_and(lax.rem(q, 2) == parity, q != l))
        def _():
            for s in range(nr):
                y_copy(q, s).wait_send()

        return carry

    lax.fori_loop(0, nc, drain, 0)


def fused_shards(sizes, ks_owned, owned_rows, left_cols, right_blocks, right_cols, kept_cols):
    nr, nc, nl = sizes
    slots, kal, bs, _ = ks_owned.shape
    limit = slots // nr
    panel = left_cols.shape[0]
    cell = panel // nc
    rrows, kbc = right_blocks.shape[:2]
    inner = rrows * nr
    kcc = kept_cols.shape[1]
    cols = inner * nl // nc
    chunk = limit * (kal // 2) * bs
    share = limit * (kcc // 2)
    f32, bf16 = jnp.float32, jnp.bfloat16
    smem = pl.BlockSpec(memory_space=pltpu.SMEM)
    vmem = pl.BlockSpec(memory_space=pltpu.VMEM)
    dma = pltpu.SemaphoreType.DMA
    return pl.pallas_call(
        functools.partial(kernel, sizes),
        out_shape=jax.ShapeDtypeStruct((cell, kcc, bs, bs), f32),
        in_specs=[smem] * 4 + [vmem] * 2,
        out_specs=vmem,
        scratch_shapes=[
            pltpu.VMEM((nr, nc, -(-slots // SUBLANES) * SUBLANES, LANES), jnp.int32),
            pltpu.SMEM((nr, nc, -(-slots // SUBLANES) * SUBLANES, LANES), jnp.int32),
            pltpu.SMEM((nc * nr, limit * (inner + kcc)), jnp.int32),
            pltpu.VMEM((nr - 1, chunk, LANES), f32),
            pltpu.VMEM((nc, nr, chunk, LANES), f32),
            pltpu.VMEM((nr, rrows * (kbc // 2) * bs, LANES), f32),
            pltpu.VMEM((inner, kbc + 1, bs, LANES), f32),
            pltpu.VMEM((inner * bs, cols * bs), bf16),
            pltpu.VMEM((inner * bs, cols * bs), bf16),
            pltpu.VMEM((limit, kal + 1, bs, LANES), f32),
            pltpu.VMEM((2 * limit * bs, inner * bs), bf16),
            pltpu.VMEM((cols, limit * bs, LANES), f32),
            pltpu.VMEM((nc, nr, share, bs, LANES), f32),
            pltpu.VMEM((nl // 2, nr, share, bs, LANES), f32),
            pltpu.VMEM((nl // 2, nr, share, bs, LANES), f32),
            dma((nr * nc - 1,)),
            dma((nr, nc)),
            dma(()),
            dma((nr - 1,)),
            dma((nr - 1,)),
            dma((2, nc, nr)),
            dma((nl // 2, nr)),
            dma((nl // 2, nr)),
            dma((nc, nr)),
            dma((nr,)),
            dma((nl // 2, nr)),
            dma((nl // 2, nr)),
        ],
        compiler_params=pltpu.CompilerParams(
            collective_id=0, has_side_effects=True, vmem_limit_bytes=60 << 20
        ),
    )(owned_rows, left_cols.T, right_cols.T, kept_cols.T, ks_owned, right_blocks)


def solution(mesh):
    sizes = (mesh.shape["row"], mesh.shape["col"], mesh.shape["layer"])
    nr, nc, nl = sizes

    def shards(ks_owned, owned_rows, left_cols, right_blocks, right_cols, kept_cols):
        bs = ks_owned.shape[2]
        inner = right_cols.shape[0]
        cols = inner * nl // nc
        even = all(v % 2 == 0 for v in (ks_owned.shape[1], right_cols.shape[1], kept_cols.shape[1], inner, cols, nl))
        fits = 4 * inner * cols * bs * bs <= DENSE_BYTES
        if 2 * bs == LANES and even and fits and nc == nl and nc > 1 and nr > 1:
            return fused_shards(sizes, ks_owned, owned_rows, left_cols, right_blocks, right_cols, kept_cols)
        return general_shards(ks_owned, owned_rows, left_cols, right_blocks, right_cols, kept_cols)

    placed = (
        P(("row", "col"), "layer", None, None),
        P(("row", "col")),
        P("row", "layer"),
        P(("layer", "row"), "col", None, None),
        P("layer", "col"),
        P("row", "col"),
    )
    return jax.shard_map(
        shards,
        mesh=mesh,
        in_specs=placed,
        out_specs=P(("row", "layer"), "col", None, None),
        check_vma=False,
    )
```

```python
import functools

import jax
import jax.numpy as jnp
from jax import lax
from jax.experimental import pallas as pl
from jax.experimental.pallas import tpu as pltpu
from jax.sharding import PartitionSpec as P

MESH = pl.DeviceIdType.MESH
LANES = 128
SUBLANES = 8
DENSE_BYTES = 8 << 20


def pack_rows(values, row_ids, groups, per_group, row_span):
    usable = row_ids >= 0
    target_group = jnp.where(usable, row_ids // row_span, groups)
    member = (target_group[:, None] == jnp.arange(groups)[None, :]).astype(jnp.int32)
    before = jnp.sum((jnp.cumsum(member, axis=0) - 1) * member, axis=1)
    target = jnp.where(usable, target_group * per_group + before, -1)
    chooser = target[None, :] == jnp.arange(groups * per_group)[:, None]
    packed = jnp.dot(chooser.astype(jnp.float32), values, precision=lax.Precision.HIGHEST)
    packed_ids = jnp.sum(jnp.where(chooser, row_ids[None, :] + 1, 0), axis=1) - 1
    return (packed, packed_ids.astype(jnp.float32))


def place_rows(arrived, arrived_ids, first_row, row_total):
    row_ids = arrived_ids.astype(jnp.int32)
    offset = row_ids - first_row
    chooser = (offset[None, :] == jnp.arange(row_total)[:, None]) & (row_ids >= 0)[None, :]
    return jnp.dot(chooser.astype(jnp.float32), arrived, precision=lax.Precision.HIGHEST)


def general_shards(ks_owned, owned_rows, left_cols, right_blocks, right_cols, kept_cols):
    row_count = lax.axis_size("row")
    col_count = lax.axis_size("col")
    owner_slots = ks_owned.shape[0]
    slot_count = ks_owned.shape[1]
    block_size = ks_owned.shape[2]
    send_limit = owner_slots // row_count
    panel_rows = left_cols.shape[0]
    cell_size = panel_rows // col_count
    my_row = lax.axis_index("row")
    flat_values = ks_owned.reshape(owner_slots, slot_count * block_size * block_size)
    packed, packed_ids = pack_rows(flat_values, owned_rows, row_count, send_limit, panel_rows)
    arrived, arrived_ids = (
        lax.all_to_all(packed, "row", split_axis=0, concat_axis=0, tiled=True),
        lax.all_to_all(packed_ids, "row", split_axis=0, concat_axis=0, tiled=True),
    )
    my_cell = my_row * col_count + lax.axis_index("col")
    cell_blocks = place_rows(arrived, arrived_ids, my_cell * cell_size, cell_size)
    left_panel = lax.all_gather(cell_blocks, "col", axis=0, tiled=True)
    right_panel = lax.all_gather(right_blocks, "row", axis=0, tiled=True)
    inner_rows = right_panel.shape[0]
    layer_start = lax.axis_index("layer") * inner_rows
    left_rows = left_panel.reshape(panel_rows, slot_count, block_size, block_size)
    local_cols = left_cols - layer_start
    picked = right_panel[local_cols]
    picked_cols = right_cols[local_cols]
    products = jnp.einsum("rkab,rklbc->rklac", left_rows, picked, precision=lax.Precision.HIGHEST)
    matches = (picked_cols[:, :, :, None] == kept_cols[:, None, None, :]).astype(jnp.float32)
    partial_value = jnp.einsum(
        "rklq,rklac->rqac", matches, products, precision=lax.Precision.HIGHEST
    )
    return lax.psum_scatter(partial_value, "layer", scatter_dimension=0, tiled=True)


def kernel(
    sizes,
    owned_ref,
    lcols_ref,
    rcols_ref,
    kept_ref,
    ks_ref,
    right_ref,
    packed_ref,
    order_ref,
    ibuf,
    ids_smem,
    xsend,
    lbuf,
    rall,
    rpanel,
    r_hi,
    r_lo,
    lpanel,
    a_both,
    spread,
    partial,
    crecv,
    yrecv,
    i_ssem,
    i_rsem,
    t_sem,
    x_ssem,
    r_ssem,
    z_ssem,
    c_ssem,
    y_ssem,
    l_rsem,
    r_rsem,
    c_rsem,
    y_rsem,
):
    nr, nc, nl = sizes
    r, c, l = lax.axis_index("row"), lax.axis_index("col"), lax.axis_index("layer")
    slots, kal, bs, _ = ks_ref.shape
    limit = slots // nr
    panel = lcols_ref.shape[1]
    cell = panel // nc
    rrows, kbc = right_ref.shape[:2]
    inner = rrows * nr
    kcc = kept_ref.shape[0]
    cols = r_hi.shape[1] // bs
    c0 = c * cols
    l0 = l * inner
    partner = l + 1 - 2 * lax.rem(l, 2)
    parity = lax.rem(l, 2)
    half = l // 2
    low = lax.broadcasted_iota(jnp.int32, (bs, LANES), 1) < bs

    barrier = pltpu.get_barrier_semaphore()
    def peer(k):
        at = lax.rem(r * nc + c + k, nr * nc)
        return {"row": at // nc, "col": lax.rem(at, nc)}

    for k in range(1, nr * nc):
        pl.semaphore_signal(barrier, inc=1, device_id=peer(k), device_id_type=MESH)
    pl.semaphore_signal(barrier, inc=1, device_id={"layer": partner}, device_id_type=MESH)
    for u in range(1, nl // 2):
        other = lax.rem(half + u, nl // 2) * 2 + parity
        pl.semaphore_signal(barrier, inc=1, device_id={"layer": other}, device_id_type=MESH)
    expect = (nr * nc - 1) + 1 + (nl // 2 - 1)

    ids = [owned_ref[s] for s in range(slots)]

    def pack_left(target, dst):
        first = target * panel
        inside = [jnp.logical_and(v >= first, v < first + panel) for v in ids]
        rank = jnp.int32(0)
        source = [jnp.int32(0)] * limit
        for s in range(slots):
            for n in range(limit):
                hit = jnp.logical_and(inside[s], rank == n)
                source[n] = jnp.where(hit, s, source[n])
            rank = rank + jnp.where(inside[s], 1, 0)
        for n in range(limit):
            for p in range(kal // 2):
                at = (n * (kal // 2) + p) * bs
                tile = jnp.concatenate([ks_ref[source[n], 2 * p], ks_ref[source[n], 2 * p + 1]], axis=-1)
                dst[pl.ds(at, bs), :] = tile

    def i_copy(k):
        return pltpu.make_async_remote_copy(
            src_ref=ibuf.at[r, c],
            dst_ref=ibuf.at[r, c],
            send_sem=i_ssem.at[k - 1],
            recv_sem=i_rsem.at[r, c],
            device_id=peer(k),
            device_id_type=MESH,
        )

    def names_of(q, s):
        first = r * panel
        rank = jnp.int32(0)
        name = [first] * limit
        for v in range(slots):
            value = ids_smem[s, q, v, 0]
            inside = jnp.logical_and(value >= first, value < first + panel)
            for n in range(limit):
                name[n] = jnp.where(jnp.logical_and(inside, rank == n), value, name[n])
            rank = rank + jnp.where(inside, 1, 0)
        return [jnp.clip(v - first, 0, panel - 1) for v in name], rank

    def x_copy(u):
        return pltpu.make_async_remote_copy(
            src_ref=xsend.at[u - 1],
            dst_ref=lbuf.at[c, r],
            send_sem=x_ssem.at[u - 1],
            recv_sem=l_rsem.at[c, r],
            device_id={"row": lax.rem(r + u, nr)},
            device_id_type=MESH,
        )

    def r_copy(u):
        return pltpu.make_async_remote_copy(
            src_ref=rall.at[r],
            dst_ref=rall.at[r],
            send_sem=r_ssem.at[u - 1],
            recv_sem=r_rsem.at[r],
            device_id={"row": lax.rem(r + u, nr)},
            device_id_type=MESH,
        )

    def z_copy(q, s, side):
        return pltpu.make_async_remote_copy(
            src_ref=lbuf.at[q, s],
            dst_ref=lbuf.at[q, s],
            send_sem=z_ssem.at[side, q, s],
            recv_sem=l_rsem.at[q, s],
            device_id={"col": c + 1 if side == 0 else c - 1},
            device_id_type=MESH,
        )

    def arrival(buf, sem):
        return pltpu.make_async_remote_copy(
            src_ref=buf,
            dst_ref=buf,
            send_sem=sem,
            recv_sem=sem,
            device_id={"layer": partner},
            device_id_type=MESH,
        )

    def both_sides(q, s, act):
        @pl.when(jnp.logical_and(q <= c, c < nc - 1))
        def _():
            act(z_copy(q, s, 0))

        @pl.when(jnp.logical_and(q >= c, c > 0))
        def _():
            act(z_copy(q, s, 1))

    start = lambda copy: copy.start()

    def order(t):
        near = jnp.minimum(c, nc - 1 - c)
        step = (t + 1) // 2
        paired = jnp.where(lax.rem(t, 2) == 1, c - step, c + step)
        single = jnp.where(c == near, c + (t - near), c - (t - near))
        return jnp.where(t <= 2 * near, paired, single)

    def passes(q):
        return jnp.logical_or(jnp.logical_and(q < c, c < nc - 1), jnp.logical_and(q > c, c > 0))

    def forward(t):
        q = order(jnp.int32(t))

        @pl.when(passes(q))
        def _():
            for u in range(nr):
                s = lax.rem(r + u, nr)
                arrival(lbuf.at[q, s], l_rsem.at[q, s]).wait_recv()
                both_sides(q, s, start)

    for u in range(1, nr):
        pack_left(lax.rem(r + u, nr), xsend.at[u - 1])
    mark = jnp.full(ibuf.shape[2:], -1, jnp.int32)
    level = lax.broadcasted_iota(jnp.int32, ibuf.shape[2:], 0)
    for s in range(slots):
        mark = jnp.where(level == s, ids[s], mark)
    ibuf[r, c] = mark
    pl.semaphore_wait(barrier, expect)
    for u in range(1, nr):
        x_copy(u).start()
    pack_left(r, lbuf.at[c, r])
    both_sides(c, r, start)
    for k in range(1, nr * nc):
        i_copy(k).start()
    for j in range(rrows):
        for p in range(kbc // 2):
            at = (j * (kbc // 2) + p) * bs
            rall[r, pl.ds(at, bs), :] = jnp.concatenate([right_ref[j, 2 * p], right_ref[j, 2 * p + 1]], axis=-1)
    for u in range(1, nr):
        r_copy(u).start()
    zero = jnp.zeros((bs, LANES), jnp.float32)

    def dense_right(s):
        def body(jj, carry):
            j = s * rrows + jj
            for p in range(kbc // 2):
                at = pl.multiple_of((jj * (kbc // 2) + p) * bs, bs)
                tile = rall[s, pl.ds(at, bs), :]
                rpanel[j, 2 * p] = tile
                rpanel[j, 2 * p + 1] = pltpu.roll(tile, bs, 1)
            rpanel[j, kbc] = zero
            names = [rcols_ref[k, j] - c0 for k in range(kbc)]
            for m in range(cols // 2):
                first, second = jnp.int32(kbc), jnp.int32(kbc)
                for k in range(kbc):
                    first = jnp.where(names[k] == 2 * m, k, first)
                    second = jnp.where(names[k] == 2 * m + 1, k ^ 1, second)
                tile = jnp.where(low, rpanel[j, first], rpanel[j, second])
                hi = tile.astype(jnp.bfloat16)
                at = pl.multiple_of(j * bs, bs)
                r_hi[pl.ds(at, bs), pl.ds(m * LANES, LANES)] = hi
                r_lo[pl.ds(at, bs), pl.ds(m * LANES, LANES)] = (tile - hi.astype(jnp.float32)).astype(jnp.bfloat16)
            return carry

        lax.fori_loop(0, rrows, body, 0)

    dense_right(r)
    for u in range(1, nr):
        s = lax.rem(r + u, nr)
        arrival(lbuf.at[c, s], l_rsem.at[c, s]).wait_recv()
        both_sides(c, s, start)
    for k in range(1, nr * nc):
        at = lax.rem(r * nc + c + k, nr * nc)
        s, q = at // nc, lax.rem(at, nc)
        arrival(ibuf.at[s, q], i_rsem.at[s, q]).wait_recv()
    table = pltpu.make_async_copy(ibuf, ids_smem, t_sem)
    table.start()
    table.wait()
    for t in range(1, min(3, nc)):
        forward(t)
    for u in range(1, nr):
        s = lax.rem(r + u, nr)
        arrival(rall.at[s], r_rsem.at[s]).wait_recv()
        dense_right(s)

    width = 2 * LANES if (cols * bs) % (2 * LANES) == 0 else LANES
    cpair = kcc // 2

    def c_copy(q, s):
        return pltpu.make_async_remote_copy(
            src_ref=partial.at[q, s],
            dst_ref=crecv.at[q // 2, s],
            send_sem=c_ssem.at[q // 2, s],
            recv_sem=c_rsem.at[q // 2, s],
            device_id={"layer": partner},
            device_id_type=MESH,
        )

    def y_copy(q, s):
        return pltpu.make_async_remote_copy(
            src_ref=partial.at[q, s],
            dst_ref=yrecv.at[half, s],
            send_sem=y_ssem.at[q // 2, s],
            recv_sem=y_rsem.at[half, s],
            device_id={"layer": q},
            device_id_type=MESH,
        )

    def chosen(table, k, q, row):
        value = table[k, q * cell]
        for i in range(1, cell):
            value = jnp.where(row == q * cell + i, table[k, q * cell + i], value)
        return value

    def product(q, s):
        rows, _ = names_of(q, s)
        for n in range(limit):
            for p in range(kal // 2):
                tile = lbuf[q, s, pl.ds((n * (kal // 2) + p) * bs, bs), :]
                lpanel[n, 2 * p] = tile
                lpanel[n, 2 * p + 1] = pltpu.roll(tile, bs, 1)
            lpanel[n, kal] = zero
            names = [chosen(lcols_ref, k, q, rows[n]) - l0 for k in range(kal)]
            for m in range(inner // 2):
                first, second = jnp.int32(kal), jnp.int32(kal)
                for k in range(kal):
                    first = jnp.where(names[k] == 2 * m, k, first)
                    second = jnp.where(names[k] == 2 * m + 1, k ^ 1, second)
                tile = jnp.where(low, lpanel[n, first], lpanel[n, second])
                hi = tile.astype(jnp.bfloat16)
                at = pl.ds(m * LANES, LANES)
                a_both[n * bs : (n + 1) * bs, at] = hi
                a_both[(limit + n) * bs : (limit + n + 1) * bs, at] = (tile - hi.astype(jnp.float32)).astype(jnp.bfloat16)
        tall = limit * bs
        dot = functools.partial(jnp.dot, preferred_element_type=jnp.float32)
        for n in range(cols * bs // width):
            at = pl.ds(n * width, width)
            value = dot(a_both[...], r_hi[:, at])
            value = value[:tall] + value[tall:] + dot(a_both[:tall, :], r_lo[:, at])
            for h in range(width // LANES):
                m = n * (width // LANES) + h
                tile = value[:, h * LANES : (h + 1) * LANES]
                spread[2 * m] = tile
                spread[2 * m + 1] = pltpu.roll(tile, bs, 1)
        for n in range(limit):
            at = pl.ds(n * bs, bs)
            for p in range(cpair):
                first = jnp.clip(chosen(kept_ref, 2 * p, q, rows[n]) - c0, 0, cols - 1)
                second = jnp.clip(chosen(kept_ref, 2 * p + 1, q, rows[n]) - c0, 0, cols - 1)
                second = second + 1 - 2 * lax.rem(second, 2)
                partial[q, s, n * cpair + p] = jnp.where(low, spread[first, at, :], spread[second, at, :])

    def step(w, carry):
        t = w // nr
        u = lax.rem(w, nr)
        q = order(t)
        s = lax.rem(r + u, nr)

        @pl.when(jnp.logical_and(q != c, jnp.logical_not(passes(q))))
        def _():
            arrival(lbuf.at[q, s], l_rsem.at[q, s]).wait_recv()

        product(q, s)

        @pl.when(lax.rem(q, 2) != parity)
        def _():
            c_copy(q, s).start()

        @pl.when(jnp.logical_and(u == nr - 1, t + 3 < nc))
        def _():
            forward(t + 3)

        @pl.when(lax.rem(q, 2) == parity)
        def _():
            arrival(crecv.at[q // 2, s], c_rsem.at[q // 2, s]).wait_recv()
            partial[q, s] = partial[q, s] + crecv[q // 2, s]

            @pl.when(q != l)
            def _():
                y_copy(q, s).start()

        return carry

    lax.fori_loop(0, nc * nr, step, 0)

    source = [jnp.int32(0)] * cell
    for s in range(nr):
        rows, count = names_of(l, s)
        for n in range(limit):
            for i in range(cell):
                hit = jnp.logical_and(rows[n] == l * cell + i, n < count)
                source[i] = jnp.where(hit, s * limit + n, source[i])
    for u in range(1, nl // 2):
        h = lax.rem(half + u, nl // 2)
        for v in range(nr):
            s = lax.rem(r + v, nr)
            arrival(yrecv.at[h, s], y_rsem.at[h, s]).wait_recv()
    for i in range(cell):
        order_ref[i] = source[i]
    for s in range(nr):
        for k in range(limit * cpair):
            tile = partial[l, s, k]
            for u in range(1, nl // 2):
                tile = tile + yrecv[lax.rem(half + u, nl // 2), s, k]
            packed_ref[s * limit * cpair + k] = tile

    wait = lambda copy: copy.wait_send()
    for u in range(1, nr):
        x_copy(u).wait_send()
        r_copy(u).wait_send()
    for k in range(1, nr * nc):
        i_copy(k).wait_send()

    def drain(q, carry):
        for s in range(nr):
            both_sides(q, s, wait)

        @pl.when(lax.rem(q, 2) != parity)
        def _():
            for s in range(nr):
                c_copy(q, s).wait_send()

        @pl.when(jnp.logical_and(lax.rem(q, 2) == parity, q != l))
        def _():
            for s in range(nr):
                y_copy(q, s).wait_send()

        return carry

    lax.fori_loop(0, nc, drain, 0)


def ordered(order_ref, packed_ref, out_ref):
    cell, kcc, bs, _ = out_ref.shape
    for i in range(cell):
        for p in range(kcc // 2):
            tile = packed_ref[order_ref[i] * (kcc // 2) + p]
            out_ref[i, 2 * p] = tile[:, :bs]
            out_ref[i, 2 * p + 1] = tile[:, bs:]


def fused_shards(sizes, ks_owned, owned_rows, left_cols, right_blocks, right_cols, kept_cols):
    nr, nc, nl = sizes
    slots, kal, bs, _ = ks_owned.shape
    limit = slots // nr
    panel = left_cols.shape[0]
    cell = panel // nc
    rrows, kbc = right_blocks.shape[:2]
    inner = rrows * nr
    kcc = kept_cols.shape[1]
    cols = inner * nl // nc
    chunk = limit * (kal // 2) * bs
    share = limit * (kcc // 2)
    f32, bf16 = jnp.float32, jnp.bfloat16
    smem = pl.BlockSpec(memory_space=pltpu.SMEM)
    vmem = pl.BlockSpec(memory_space=pltpu.VMEM)
    dma = pltpu.SemaphoreType.DMA
    packed, order = pl.pallas_call(
        functools.partial(kernel, sizes),
        out_shape=(jax.ShapeDtypeStruct((nr * share, bs, LANES), f32), jax.ShapeDtypeStruct((cell,), jnp.int32)),
        in_specs=[smem] * 4 + [vmem] * 2,
        out_specs=(vmem, smem),
        scratch_shapes=[
            pltpu.VMEM((nr, nc, -(-slots // SUBLANES) * SUBLANES, LANES), jnp.int32),
            pltpu.SMEM((nr, nc, -(-slots // SUBLANES) * SUBLANES, LANES), jnp.int32),
            pltpu.VMEM((nr - 1, chunk, LANES), f32),
            pltpu.VMEM((nc, nr, chunk, LANES), f32),
            pltpu.VMEM((nr, rrows * (kbc // 2) * bs, LANES), f32),
            pltpu.VMEM((inner, kbc + 1, bs, LANES), f32),
            pltpu.VMEM((inner * bs, cols * bs), bf16),
            pltpu.VMEM((inner * bs, cols * bs), bf16),
            pltpu.VMEM((limit, kal + 1, bs, LANES), f32),
            pltpu.VMEM((2 * limit * bs, inner * bs), bf16),
            pltpu.VMEM((cols, limit * bs, LANES), f32),
            pltpu.VMEM((nc, nr, share, bs, LANES), f32),
            pltpu.VMEM((nl // 2, nr, share, bs, LANES), f32),
            pltpu.VMEM((nl // 2, nr, share, bs, LANES), f32),
            dma((nr * nc - 1,)),
            dma((nr, nc)),
            dma(()),
            dma((nr - 1,)),
            dma((nr - 1,)),
            dma((2, nc, nr)),
            dma((nl // 2, nr)),
            dma((nl // 2, nr)),
            dma((nc, nr)),
            dma((nr,)),
            dma((nl // 2, nr)),
            dma((nl // 2, nr)),
        ],
        compiler_params=pltpu.CompilerParams(
            collective_id=0, has_side_effects=True, vmem_limit_bytes=60 << 20
        ),
    )(owned_rows, left_cols.T, right_cols.T, kept_cols.T, ks_owned, right_blocks)
    return pl.pallas_call(
        ordered,
        out_shape=jax.ShapeDtypeStruct((cell, kcc, bs, bs), f32),
        in_specs=[smem, vmem],
        out_specs=vmem,
    )(order, packed)


def solution(mesh):
    sizes = (mesh.shape["row"], mesh.shape["col"], mesh.shape["layer"])
    nr, nc, nl = sizes

    def shards(ks_owned, owned_rows, left_cols, right_blocks, right_cols, kept_cols):
        bs = ks_owned.shape[2]
        inner = right_cols.shape[0]
        cols = inner * nl // nc
        even = all(v % 2 == 0 for v in (ks_owned.shape[1], right_cols.shape[1], kept_cols.shape[1], inner, cols, nl))
        fits = 4 * inner * cols * bs * bs <= DENSE_BYTES
        if 2 * bs == LANES and even and fits and nc == nl and nc > 1 and nr > 1:
            return fused_shards(sizes, ks_owned, owned_rows, left_cols, right_blocks, right_cols, kept_cols)
        return general_shards(ks_owned, owned_rows, left_cols, right_blocks, right_cols, kept_cols)

    placed = (
        P(("row", "col"), "layer", None, None),
        P(("row", "col")),
        P("row", "layer"),
        P(("layer", "row"), "col", None, None),
        P("layer", "col"),
        P("row", "col"),
    )
    return jax.shard_map(
        shards,
        mesh=mesh,
        in_specs=placed,
        out_specs=P(("row", "layer"), "col", None, None),
        check_vma=False,
    )
```
